256 devices in a mesh: gx: 16 (over y, x), gy: 16 (over z, core).
Axes of the slice: x: 4, y: 4, z: 8, core: 2. Of those that a mesh axis runs over, the one named last changes fastest.
Arguments:
- iterate: float32 [128, 256, 1024], P('gx', 'gy'), may hold values from -6 to 6
- residual: float32 [128, 256, 1024], P('gx', 'gy'), may hold values from -12 to 12
- direction: float32 [128, 256, 1024], P('gx', 'gy'), may hold values from -12 to 12
- brain_mask: int32 [128, 256, 16], P('gx', 'gy'), may hold values 0 or 1
- dictionary: float32 [90, 64], replicated, may hold values from -0.75 to 0.75
- spatial_weight: float32 [64], replicated, may hold values from 0.3 to 3
- angular_weight: float32 [64, 64], replicated, may hold values from 0 to 0.05
- orient_offsets: int32 [64, 3], replicated, may hold values from -1 to 1, as said below
Outputs:
- new_iterate: float32 [128, 256, 1024], P('gx', 'gy')
- new_residual: float32 [128, 256, 1024], P('gx', 'gy')
- new_direction: float32 [128, 256, 1024], P('gx', 'gy')
The draws below stay inside these ranges and needn't reach their ends.
Inputs may be any that keep to these rules, and one draw needn't show every extreme that they name: `orient_offsets`: each row is one of the 13 steps whose first nonzero component is 1; every one of them occurs.
All inputs are finite; a program needn't handle non-finite values. No bound on the sum of `brain_mask` on one device may be relied on, other than what follows from the above.
Results may differ from the reference program's by a relative error of at most 0.0002.
Values sent between devices are 32-bit elements; how exact they have to be, the bound alone decides.
No kernel may reach another device: no remote copies, remote signals or barrier semaphores. Data moves between devices by JAX's collectives and lax.ppermute only.
A program may use at most 64 MiB of HBM per device.

```python
import math
import jax
import jax.numpy as jnp
from jax import lax

NZ = 16
C = 64
G = 90
ITERS = 4
NX = 128
NY = 256


DIRECTIONS = [(0, 0, 1), (0, 1, -1), (0, 1, 0), (0, 1, 1), (1, -1, -1), (1, -1, 0), (1, -1, 1), (1, 0, -1), (1, 0, 0), (1, 0, 1), (1, 1, -1), (1, 1, 0), (1, 1, 1)]


def field_draw(key, salt):
    key = jax.random.fold_in(key, salt)
    key_one, key_two = jax.random.split(key)
    shape = (NX, NY, NZ * C)
    position = jax.lax.broadcasted_iota(jnp.float32, shape, 0)
    rising = 0.6 + 1.2 * position / max(NX - 1, 1)
    values = jax.random.normal(key_one, shape, jnp.float32)
    values = jnp.clip(values, -6.0, 6.0)
    return (values * rising).astype(jnp.float32)


def draw_residual(key, part):
    return field_draw(key, 11)


def draw_direction(key, part):
    return field_draw(key, 23)


def draw_orient_offsets(key, part):
    chosen = jax.random.randint(jax.random.fold_in(key, 37), (C,), 0, 13)
    counter = jnp.arange(C, dtype=jnp.int32)
    picks = jnp.where(counter < 13, counter % 13, chosen)
    table = jnp.array(DIRECTIONS, dtype=jnp.int32)
    return table[picks]


def with_ends(entries, rng, least, top_value):
    extent = entries.shape
    place = [jax.random.randint(jax.random.fold_in(rng, axis), (), 0, extent[axis]) for axis in range(len(extent))]
    entries = entries.at[tuple(place)].set(least)
    longest = extent.index(max(extent))
    place[longest] = (place[longest] + 1) % extent[longest]
    return entries.at[tuple(place)].set(top_value)


def levels(own_key, dims, cuts, smallest, largest):
    def one(dim, shards_of):
        draws = jax.random.uniform(jax.random.fold_in(jax.random.fold_in(own_key, 6), dim), (shards_of,), jnp.float32, smallest / len(cuts), largest / len(cuts))
        return jnp.repeat(jnp.exp(draws), dims[dim] // shards_of).reshape((-1,) + (1,) * (len(dims) - dim - 1))

    loudness = one(*cuts[0])
    for cut in cuts[1:]:
        loudness = loudness * one(*cut)
    return loudness


def normal_values(rng, shape, scale, reach, shards=(), kind=jnp.bfloat16):
    factor_of = levels(rng, shape, shards, -0.22, 0.18) if shards else 1.0
    entries = jax.random.normal(rng, shape, jnp.float32) * scale * factor_of
    return jnp.minimum(jnp.maximum(entries, -reach), reach).astype(kind)


def setup_inputs(seed: int = 0) -> dict:
    key_list = jax.random.split(jax.random.key(seed), 9)
    iterate = normal_values(key_list[0], (NX, NY, NZ * C), 1.0, 6.0, ((0, 16), (1, 16)), jnp.float32)
    residual = draw_residual(jax.random.fold_in(key_list[8], 71), 0)
    direction = draw_direction(jax.random.fold_in(key_list[8], 71), 0)
    brain_mask = with_ends((jax.random.randint(key_list[3], (NX, NY, NZ), 0, 4) < 3).astype(jnp.int32), jax.random.fold_in(key_list[3], 1), 0, 1)
    dictionary = normal_values(key_list[4], (G, C), C ** -0.5, 0.75, (), jnp.float32)
    spatial_weight = jnp.clip(jnp.exp(jax.random.uniform(key_list[5], (C,), jnp.float32, math.log(0.3), math.log(3.0))), 0.3, 3.0)
    angular_weight = jnp.clip(jax.random.uniform(key_list[6], (C, C), jnp.float32, 0.0, 0.05), 0.0, 0.05)
    orient_offsets = draw_orient_offsets(jax.random.fold_in(key_list[8], 71), 0)
    return dict(iterate=iterate, residual=residual, direction=direction, brain_mask=brain_mask, dictionary=dictionary, spatial_weight=spatial_weight, angular_weight=angular_weight, orient_offsets=orient_offsets)


DIRECTIONS = [(0, 0, 1), (0, 1, -1), (0, 1, 0), (0, 1, 1), (1, -1, -1), (1, -1, 0), (1, -1, 1), (1, 0, -1), (1, 0, 0), (1, 0, 1), (1, 1, -1), (1, 1, 0), (1, 1, 1)]


def angular_matrix(angular_weight):
    symmetric = 0.5 * (angular_weight + angular_weight.T)
    channels = symmetric.shape[0]
    coupling = symmetric * (1.0 - jnp.eye(channels, dtype=jnp.float32))
    return jnp.diag(jnp.sum(coupling, axis=1)) - coupling


def channel_selector(orient_offsets):
    table = jnp.array(DIRECTIONS, dtype=jnp.int32)
    hits = jnp.all(orient_offsets[None, :, :] == table[:, None, :], axis=-1)
    return hits.astype(jnp.float32)


def neighbour_sum(extended, selector, width_x, width_y, depth, channels):
    padded = jnp.pad(extended, ((0, 0), (0, 0), (channels, channels)))
    running_sum = jnp.zeros((width_x, width_y, depth), jnp.float32)
    slices = depth // channels
    for number in range(len(DIRECTIONS)):
        step_x, step_y, step_z = DIRECTIONS[number]
        forward = padded[1 + step_x:1 + step_x + width_x, 1 + step_y:1 + step_y + width_y, channels + step_z * channels:channels + step_z * channels + depth]
        backward = padded[1 - step_x:1 - step_x + width_x, 1 - step_y:1 - step_y + width_y, channels - step_z * channels:channels - step_z * channels + depth]
        running_sum = running_sum + jnp.tile(selector[number], slices) * (forward + backward)
    return running_sum


def apply_operator(field_data, extended, brain_mask, dictionary, spatial_weight, angular_full, selector):
    width_x, width_y, depth = field_data.shape
    channels = dictionary.shape[1]
    flattened = field_data.reshape(-1, channels)
    signal = jnp.dot(flattened, dictionary.T, precision=lax.Precision.HIGHEST, preferred_element_type=jnp.float32)
    back_proj = jnp.dot(signal, dictionary, precision=lax.Precision.HIGHEST, preferred_element_type=jnp.float32)
    mask_rows = brain_mask.reshape(-1).astype(jnp.float32)
    data_term = (back_proj * mask_rows[:, None]).reshape(width_x, width_y, depth)
    angular_term = jnp.dot(flattened, angular_full, precision=lax.Precision.HIGHEST, preferred_element_type=jnp.float32).reshape(width_x, width_y, depth)
    neighbours = neighbour_sum(extended, selector, width_x, width_y, depth, channels)
    spatial_rows = jnp.tile(spatial_weight, depth // channels)
    return data_term + angular_term + spatial_rows * (2.0 * field_data - neighbours)


def reference(iterate, residual, direction, brain_mask, dictionary, spatial_weight, angular_weight, orient_offsets):
    angular_full = angular_matrix(angular_weight)
    selector = channel_selector(orient_offsets)
    norm_now = jnp.sum(residual * residual)
    for iteration_number in range(ITERS):
        extended = jnp.pad(direction, ((1, 1), (1, 1), (0, 0)))
        images = apply_operator(direction, extended, brain_mask, dictionary, spatial_weight, angular_full, selector)
        step_length = norm_now / jnp.sum(direction * images)
        iterate = iterate + step_length * direction
        residual = residual - step_length * images
        norm_next = jnp.sum(residual * residual)
        direction = residual + (norm_next / norm_now) * direction
        norm_now = norm_next
    return iterate, residual, direction
```

```python
import functools

import jax
import jax.numpy as jnp
from jax import lax
from jax.experimental import pallas as pl
from jax.experimental.pallas import tpu as pltpu
from jax.sharding import PartitionSpec as P

ITERS = 4
AXES = ("gx", "gy")
AMPLIFICATION_LIMIT = 200.0
F32 = jnp.float32
BF16 = jnp.bfloat16

DIRECTIONS = [
    (0, 0, 1),
    (0, 1, -1),
    (0, 1, 0),
    (0, 1, 1),
    (1, -1, -1),
    (1, -1, 0),
    (1, -1, 1),
    (1, 0, -1),
    (1, 0, 0),
    (1, 0, 1),
    (1, 1, -1),
    (1, 1, 0),
    (1, 1, 1),
]

WX, WY = 8, 16
DEEP = 4
FX, FY = WX + 2 * DEEP, WY + 2 * DEEP
Y_TILES = WX * (DEEP + DEEP - 1) + 1
X_TILES = WY * (DEEP + DEEP - 1) + 2
C_TILES = DEEP * 2 * DEEP + (DEEP - 1) * 2 * (DEEP - 1) + 2
MOMENTS = 24


def padded_2(cells, sides, width):
    for axis, dim in sides:
        count = lax.axis_size(axis)
        ends = count - 1
        head = lax.slice_in_dim(cells, 0, width, axis=dim)
        tail = lax.slice_in_dim(cells, cells.shape[dim] - width, cells.shape[dim], axis=dim)
        cells = jnp.concatenate(
            [
                lax.ppermute(tail, axis, [(i, (i + 1) % count) for i in range(ends)]),
                cells,
                lax.ppermute(head, axis, [((i + 1) % count, i) for i in range(ends)]),
            ],
            axis=dim,
        )
    return cells


def angular_matrix(angular_weight):
    symmetric = 0.5 * (angular_weight + angular_weight.T)
    channels = symmetric.shape[0]
    coupling = symmetric * (1.0 - jnp.eye(channels, dtype=jnp.float32))
    return jnp.diag(jnp.sum(coupling, axis=1)) - coupling


def channel_selector(orient_offsets):
    table = jnp.array(DIRECTIONS, dtype=jnp.int32)
    hits = jnp.all(orient_offsets[None, :, :] == table[:, None, :], axis=-1)
    return hits.astype(jnp.float32)


def neighbour_sum(extended, selector, width_x, width_y, depth, channels):
    padded = jnp.pad(extended, ((0, 0), (0, 0), (channels, channels)))
    running_sum = jnp.zeros((width_x, width_y, depth), jnp.float32)
    slices = depth // channels
    for number in range(len(DIRECTIONS)):
        step_x, step_y, step_z = DIRECTIONS[number]
        forward = padded[
            1 + step_x : 1 + step_x + width_x,
            1 + step_y : 1 + step_y + width_y,
            channels + step_z * channels : channels + step_z * channels + depth,
        ]
        backward = padded[
            1 - step_x : 1 - step_x + width_x,
            1 - step_y : 1 - step_y + width_y,
            channels - step_z * channels : channels - step_z * channels + depth,
        ]
        running_sum = running_sum + jnp.tile(selector[number], slices) * (forward + backward)
    return running_sum


def apply_operator(field_data, brain_mask, dictionary, spatial_rows, angular_full, selector):
    extended = padded_2(field_data, (("gx", 0), ("gy", 1)), 1)
    width_x, width_y, depth = field_data.shape
    channels = dictionary.shape[1]
    flattened = field_data.reshape(-1, channels)
    dot = functools.partial(
        jnp.dot, precision=lax.Precision.HIGHEST, preferred_element_type=jnp.float32
    )
    back_proj = dot(dot(flattened, dictionary.T), dictionary)
    mask_rows = brain_mask.reshape(-1).astype(jnp.float32)
    data_term = (back_proj * mask_rows[:, None]).reshape(width_x, width_y, depth)
    angular_term = dot(flattened, angular_full).reshape(width_x, width_y, depth)
    neighbours = neighbour_sum(extended, selector, width_x, width_y, depth, channels)
    return data_term + angular_term + spatial_rows * (2.0 * field_data - neighbours)


def plain_recurrence(
    iterate, residual, direction, brain_mask, dictionary, spatial_weight, angular_weight, offsets
):
    angular_full = angular_matrix(angular_weight)
    selector = channel_selector(offsets)
    spatial_rows = jnp.tile(spatial_weight, iterate.shape[2] // dictionary.shape[1])

    def step(_, state):
        iterate, residual, direction, norm_now = state
        images = apply_operator(
            direction, brain_mask, dictionary, spatial_rows, angular_full, selector
        )
        curvature = lax.psum(jnp.sum(direction * images), AXES)
        step_length = norm_now / curvature
        iterate = iterate + step_length * direction
        residual = residual - step_length * images
        norm_next = lax.psum(jnp.sum(residual * residual), AXES)
        direction = residual + norm_next / norm_now * direction
        return iterate, residual, direction, norm_next

    norm = lax.psum(jnp.sum(residual * residual), AXES)
    state = lax.fori_loop(0, ITERS, step, (iterate, residual, direction, norm))
    return state[:3]


def pack_kernel(d_ref, r_ref, m_ref, dc, rc, mrow, ylo, yhi, xlo, xhi):
    for src, dst in ((d_ref, dc), (r_ref, rc)):
        for x in range(WX):
            for half in range(2):
                for k in range(8):
                    tile = src[x, 8 * half : 8 * half + 8, 128 * k : 128 * k + 128]
                    dst[pl.ds((x * WY + 8 * half) * 8 + k, 8, stride=8), :] = tile
    for y in range(WY):
        lane = 16 * (y % 8)
        mrow[8 * (y // 8) : 8 * (y // 8) + 8, lane : lane + 16] = m_ref[:, y, :].astype(F32)
    base = 8 * WX * DEEP
    for x in range(WX):
        row = x * WY * 8
        for src, wide, at in ((dc, DEEP, 0), (rc, DEEP - 1, base)):
            n = 8 * wide
            ylo[at + x * n : at + x * n + n, :] = src[row : row + n, :]
            yhi[at + x * n : at + x * n + n, :] = src[row + WY * 8 - n : row + WY * 8, :]
    last = 8 * (Y_TILES - 1)
    ylo[last:, :] = mrow[0:8, :]
    yhi[last:, :] = mrow[8:16, :]
    at = 0
    for src, wide in ((dc, DEEP), (rc, DEEP - 1)):
        n = 8 * WY * wide
        xlo[at : at + n, :] = src[0:n, :]
        xhi[at : at + n, :] = src[8 * WX * WY - n :, :]
        at += n
    xlo[at:, :] = mrow[...]
    xhi[at:, :] = mrow[...]


def corner_kernel(left, right, clo, chi):
    at = 0
    base = 0
    for wide in (DEEP, DEEP - 1):
        n = 8 * wide
        for i in range(wide):
            for out, x in ((clo, i), (chi, WX - wide + i)):
                out[at : at + n, :] = left[base + x * n : base + x * n + n, :]
                out[at + n : at + 2 * n, :] = right[base + x * n : base + x * n + n, :]
            at += 2 * n
        base += WX * n
    for out in (clo, chi):
        out[at : at + 8, :] = left[base : base + 8, :]
        out[at + 8 : at + 16, :] = right[base : base + 8, :]


def weights_kernel(dict_ref, ang_ref, angt_ref, sw_ref, w_hi, w_lo, par, wide):
    dictionary = dict_ref[...]
    gram = lax.dot_general(
        dictionary,
        dictionary,
        (((0,), (0,)), ((), ())),
        precision=lax.Precision.HIGHEST,
        preferred_element_type=F32,
    )
    row = lax.broadcasted_iota(jnp.int32, (64, 64), 0)
    col = lax.broadcasted_iota(jnp.int32, (64, 64), 1)
    same = row == col
    coupling = jnp.where(same, 0.0, 0.5 * (ang_ref[...] + angt_ref[...]))
    degree = jnp.sum(coupling, axis=0, keepdims=True)
    weight = sw_ref[:, 0:64]
    angular = jnp.where(same, degree, 0.0) - coupling
    size = jnp.sum(jnp.abs(gram), axis=0, keepdims=True) + 2.0 * degree + 4.0 * weight
    scale = jnp.max(size, axis=1, keepdims=True)
    centre = jnp.sum(jnp.where(same, gram, 0.0), axis=0, keepdims=True) + degree + 2.0 * weight
    shift = jnp.sum(centre, axis=1, keepdims=True) * (1.0 / 64.0)
    inverse = 1.0 / scale
    first = gram * inverse
    second = (angular + jnp.where(same, 2.0 * weight - shift, 0.0)) * inverse
    wide[...] = jnp.zeros_like(wide)
    for half in range(2):
        at = 64 * half
        wide[at : at + 64, at : at + 64] = first
        wide[at : at + 64, 128 + at : 128 + at + 64] = second
    full = wide[...]
    high = full.astype(BF16)
    low = (full - high.astype(F32)).astype(BF16)
    w_hi[0:128, :] = high
    w_hi[128:256, :] = high
    w_lo[0:128, :] = low
    w_lo[128:256, :] = low
    par[0:8, :] = jnp.broadcast_to(sw_ref[...] * inverse, (8, 128))
    par[8:16, :] = jnp.broadcast_to(scale, (8, 128))
    par[16:24, :] = jnp.broadcast_to(shift, (8, 128))


def krylov_kernel(
    dc, rc, mrow, yl, yr, xl, xr, cl, cr, w_hi, w_lo, par, off,
    d1o, d2o, d3o, d4o, r1o, r2o, r3o, part,
    d0, d1, d2, d3, d4, r0, r1, r2, r3, me, qf, qb, tiles, lhs, in_sem, out_sem,
):
    copies = []

    def fetch(src, dst):
        copy = pltpu.make_async_copy(src, dst, in_sem)
        copy.start()
        copies.append(copy)

    own_x, own_y = pl.ds(DEEP, WX), pl.ds(DEEP, WY)
    fetch(dc, d0.at[own_x, own_y])
    fetch(rc, r0.at[own_x, own_y])
    for wide, field, base, xbase, cbase in (
        (DEEP, d0, 0, 0, 0),
        (DEEP - 1, r0, WX * DEEP, WY * DEEP, 2 * DEEP * DEEP),
    ):
        lo, hi_y, hi_x = DEEP - wide, DEEP + WY, DEEP + WX
        for x in range(WX):
            fetch(yl.at[pl.ds(base + wide * x, wide)], field.at[DEEP + x, pl.ds(lo, wide)])
            fetch(yr.at[pl.ds(base + wide * x, wide)], field.at[DEEP + x, pl.ds(hi_y, wide)])
        for i in range(wide):
            for block, corner, x in ((xl, cl, lo + i), (xr, cr, hi_x + i)):
                fetch(block.at[pl.ds(xbase + WY * i, WY)], field.at[x, own_y])
                at = cbase + 2 * wide * i
                fetch(corner.at[pl.ds(at, wide)], field.at[x, pl.ds(lo, wide)])
                fetch(corner.at[pl.ds(at + wide, wide)], field.at[x, pl.ds(hi_y, wide)])
    fetch(yl.at[pl.ds(Y_TILES - 1, 1)], tiles.at[pl.ds(0, 1)])
    fetch(mrow, tiles.at[pl.ds(1, 2)])
    fetch(yr.at[pl.ds(Y_TILES - 1, 1)], tiles.at[pl.ds(3, 1)])
    for at, block, corner in ((4, xl, cl), (8, xr, cr)):
        fetch(corner.at[pl.ds(C_TILES - 2, 1)], tiles.at[pl.ds(at, 1)])
        fetch(block.at[pl.ds(X_TILES - 2, 2)], tiles.at[pl.ds(at + 1, 2)])
        fetch(corner.at[pl.ds(C_TILES - 1, 1)], tiles.at[pl.ds(at + 3, 1)])

    sub = lax.broadcasted_iota(jnp.int32, (8, 128), 0)
    lane = lax.broadcasted_iota(jnp.int32, (8, 128), 1)
    off_x = jnp.broadcast_to(off[0:1, :], (8, 128))
    off_y = jnp.broadcast_to(off[1:2, :], (8, 128))
    off_z = jnp.broadcast_to(off[2:3, :], (8, 128))
    lower = lane < 64
    flat_z = off_z == 0
    direct = jnp.logical_or(
        jnp.logical_and(lower, off_z == 1), jnp.logical_and(lane >= 64, off_z == -1)
    )
    edge = jnp.logical_or(
        jnp.logical_and(lower, sub == 0), jnp.logical_and(lane >= 64, sub == 7)
    )
    inside = jnp.where(edge, 0.0, 1.0).astype(F32)
    y_minus, y_plus, x_step = off_y == -1, off_y == 1, off_x == 1
    weight = par[0:8, :]

    for copy in copies:
        copy.wait()

    for frame_y in range(1, FY - 1):
        y = frame_y - DEEP + 8
        group, amount = y // 8, 16 * (y % 8)
        column = jnp.concatenate(
            [tiles[4 + group][4:8], tiles[group], tiles[8 + group][0:4]], axis=0
        )
        if amount:
            column = pltpu.roll(column, 128 - amount, 1)
        lhs[pl.ds(frame_y, FX, stride=FY), :] = column
    slots = lhs[...].astype(BF16)
    z_row = lax.broadcasted_iota(jnp.int32, (128, 128), 0)
    z_lane = lax.broadcasted_iota(jnp.int32, (128, 128), 1) // 64
    for k in range(8):
        spread = jnp.where(z_row == 2 * k + z_lane, 1.0, 0.0).astype(BF16)
        me[pl.ds(k, FX * FY, stride=8), :] = jnp.dot(
            slots, spread, preferred_element_type=F32
        )

    gx, gy = lax.axis_index("gx"), lax.axis_index("gy")
    ends_x, ends_y = lax.axis_size("gx") - 1, lax.axis_size("gy") - 1

    def operator(src, dst, depth):
        lo, wide = DEEP - depth, WY + 2 * depth
        inner = wide - 2

        def shift_row(x, _):
            v = src[x, pl.ds(lo, wide)]
            rot = pltpu.roll(v, 64, 2)
            far = jnp.where(lower, pltpu.roll(rot, 1, 1), pltpu.roll(rot, 7, 1)) * inside
            u = jnp.where(flat_z, v, jnp.where(direct, rot, far))
            w = jnp.where(flat_z, v, jnp.where(direct, far, rot))
            qf[x, pl.ds(lo + 1, inner)] = jnp.where(
                y_minus, u[:-2], jnp.where(y_plus, u[2:], u[1:-1])
            )
            qb[x, pl.ds(lo + 1, inner)] = jnp.where(
                y_minus, w[2:], jnp.where(y_plus, w[:-2], w[1:-1])
            )
            return 0

        lax.fori_loop(lo, FX - lo, shift_row, 0)

        def combine_row(x, _):
            cols = pl.ds(lo + 1, inner)
            v = src[x, cols].reshape(inner * 8, 128)
            high = v.astype(BF16)
            low = (v - high.astype(F32)).astype(BF16)
            both = jnp.concatenate([high, low], axis=1)
            prod = jnp.dot(both, w_hi[...], preferred_element_type=F32)
            prod = prod + jnp.dot(both, w_lo[...], preferred_element_type=F32)
            near = jnp.where(x_step, qf[x + 1, cols], qf[x, cols])
            near = near + jnp.where(x_step, qb[x - 1, cols], qb[x, cols])
            data = prod[:, 0:128].reshape(inner, 8, 128)
            rest = prod[:, 128:256].reshape(inner, 8, 128)
            start = pl.multiple_of((x * FY + lo + 1) * 8, 8)
            mask = me[pl.ds(start, inner * 8), :].reshape(inner, 8, 128)
            dst[x, cols] = mask * data + rest - weight * near
            return 0

        lax.fori_loop(lo + 1, FX - lo - 1, combine_row, 0)

        border = depth - 1
        if border:
            zero_rows = jnp.zeros((border, inner, 8, 128), F32)
            zero_cols = jnp.zeros((WX + 2 * border, border, 8, 128), F32)
            rows, cols = pl.ds(lo + 1, FX - 2 * lo - 2), pl.ds(lo + 1, inner)

            @pl.when(gx == 0)
            def _():
                dst[pl.ds(lo + 1, border), cols] = zero_rows

            @pl.when(gx == ends_x)
            def _():
                dst[pl.ds(DEEP + WX, border), cols] = zero_rows

            @pl.when(gy == 0)
            def _():
                dst[rows, pl.ds(lo + 1, border)] = zero_cols

            @pl.when(gy == ends_y)
            def _():
                dst[rows, pl.ds(DEEP + WY, border)] = zero_cols

    stores = []

    def put(src, dst):
        copy = pltpu.make_async_copy(src.at[own_x, own_y], dst, out_sem)
        copy.start()
        stores.append(copy)

    for src, dst, out, depth in (
        (d0, d1, d1o, 4),
        (d1, d2, d2o, 3),
        (r0, r1, r1o, 3),
        (d2, d3, d3o, 2),
        (r1, r2, r2o, 2),
        (d3, d4, d4o, 1),
        (r2, r3, r3o, 1),
    ):
        operator(src, dst, depth)
        put(dst, out)

    ds, rs = (d0, d1, d2, d3, d4), (r0, r1, r2, r3)
    pairs = [(ds[k // 2], ds[k - k // 2]) for k in range(9)]
    pairs += [(rs[min(k // 2, 3)], ds[k - min(k // 2, 3)]) for k in range(8)]
    pairs += [(rs[k // 2], rs[k - k // 2]) for k in range(7)]

    def accumulate(i, acc):
        x, y = DEEP + i // 2, DEEP + 8 * (i % 2)
        cols = pl.ds(y, 8)
        loaded = {id(f): f[x, cols] for f in ds + rs}
        return tuple(
            a + jnp.sum(loaded[id(f)] * loaded[id(g)], axis=0)
            for a, (f, g) in zip(acc, pairs)
        )

    zero = jnp.zeros((8, 128), F32)
    acc = lax.fori_loop(0, 2 * WX, accumulate, (zero,) * MOMENTS)
    total = zero[0:1, :]
    lane_row = lax.broadcasted_iota(jnp.int32, (1, 128), 1)
    for k, a in enumerate(acc):
        value = jnp.sum(jnp.sum(a, axis=0, keepdims=True), axis=1, keepdims=True)
        total = jnp.where(lane_row == k, value, total)
    part[...] = jnp.broadcast_to(total, part.shape)
    for copy in stores:
        copy.wait()


def scalars_kernel(sums, par, coef, flag):
    row = jnp.sum(sums[...], axis=0, keepdims=True)
    moment = [jnp.broadcast_to(row[:, k : k + 1], (8, 128)) for k in range(MOMENTS)]
    mu, nu, rho = moment[0:9], moment[9:17], moment[17:24]
    scale = par[8:16, :]
    inverse = 1.0 / scale
    sigma = par[16:24, :] * inverse
    one, zero = jnp.ones((8, 128), F32), jnp.zeros((8, 128), F32)

    def product(p, q):
        out = [None] * max(len(p) + len(q) - 1, 0)
        for i, a in enumerate(p):
            for j, b in enumerate(q):
                out[i + j] = a * b if out[i + j] is None else out[i + j] + a * b
        return out

    def form(v, w):
        crossed = product(v[0], w[1]), product(w[0], v[1])
        total, size = zero, zero
        for c, m in ((product(v[0], w[0]), mu), (product(v[1], w[1]), rho)):
            for a, b in zip(c, m):
                total, size = total + a * b, size + jnp.abs(a * b)
        for a, b, m in zip(crossed[0], crossed[1], nu):
            total, size = total + (a + b) * m, size + (jnp.abs(a) + jnp.abs(b)) * jnp.abs(m)
        return total, size

    def add(p, factor, q):
        out = []
        for i in range(max(len(p), len(q))):
            if i >= len(q):
                out.append(p[i])
            elif i >= len(p):
                out.append(factor * q[i])
            else:
                out.append(p[i] + factor * q[i])
        return out

    def image(v):
        return tuple(add([zero] + p, sigma, p) if p else [] for p in v)

    xs, rs, ds = ([], []), ([], [one]), ([one], [])
    norm = rho[0]
    worst = zero
    for _ in range(ITERS):
        applied = image(ds)
        curvature, size = form(ds, applied)
        worst = jnp.maximum(worst, size / jnp.abs(curvature))
        bad = jnp.logical_not(size <= AMPLIFICATION_LIMIT * curvature)
        step = norm / curvature
        xs = tuple(add(p, step, q) for p, q in zip(xs, ds))
        rs = tuple(add(p, -step, q) for p, q in zip(rs, applied))
        after, size = form(rs, rs)
        bad = jnp.logical_or(bad, jnp.logical_not(size <= AMPLIFICATION_LIMIT * after))
        worst = jnp.where(bad, 2.0 * AMPLIFICATION_LIMIT, worst)
        ds = tuple(add(p, after / norm, q) for p, q in zip(rs, ds))
        norm = after
    rows = [a * inverse for a in xs[0] + xs[1]] + rs[0] + rs[1] + ds[0] + ds[1]
    for k, a in enumerate(rows):
        coef[k] = a
    flag[...] = jnp.where(worst <= AMPLIFICATION_LIMIT, 1, 0).astype(jnp.int32)


def combine_kernel(x_ref, dc, rc, d1, d2, d3, d4, r1, r2, r3, coef, xo, ro, do):
    c = [coef[k] for k in range(25)]
    fields = (dc, d1, d2, d3, d4, rc, r1, r2, r3)
    to_x = dict(zip((0, 1, 2, 3, 5, 6, 7), c[0:7]))

    def row(x, _):
        for half in range(2):
            for k in range(8):
                at = (x * WY + 8 * half) * 8 + k
                b = [f[pl.ds(at, 8, stride=8), :] for f in fields]
                place = (x, slice(8 * half, 8 * half + 8), slice(128 * k, 128 * k + 128))
                value = x_ref[place]
                for i, a in to_x.items():
                    value = value + a * b[i]
                xo[place] = value
                for out, base in ((ro, 7), (do, 16)):
                    value = c[base] * b[0]
                    for i in range(1, 9):
                        value = value + c[base + i] * b[i]
                    out[place] = value
        return 0

    lax.fori_loop(0, WX, row, 0)


def spec(space=pltpu.VMEM):
    return pl.BlockSpec(memory_space=space)


def tiles_of(n):
    return jax.ShapeDtypeStruct((n * 8, 128), F32)


def estimate(flops, bytes_accessed):
    return pl.CostEstimate(flops=flops, bytes_accessed=bytes_accessed, transcendentals=0)


def moved(value, axis, step):
    count = lax.axis_size(axis)
    pairs = [(i, i + step) for i in range(count) if 0 <= i + step < count]
    return lax.ppermute(value, axis, pairs)


def total_over(rows, axis):
    return jnp.sum(lax.all_to_all(rows, axis, 0, 0, tiled=True), axis=0, keepdims=True)


def per_device(
    iterate,
    residual,
    direction,
    brain_mask,
    dictionary,
    spatial_weight,
    angular_weight,
    orient_offsets,
):
    cells = WX * WY
    dc, rc, mrow, ylo, yhi, xlo, xhi = pl.pallas_call(
        pack_kernel,
        out_shape=(
            tiles_of(cells), tiles_of(cells), tiles_of(2), tiles_of(Y_TILES),
            tiles_of(Y_TILES), tiles_of(X_TILES), tiles_of(X_TILES),
        ),
        in_specs=[spec()] * 3,
        out_specs=[spec()] * 7,
        cost_estimate=estimate(0, 4 << 20),
        name="pack",
    )(direction, residual, brain_mask)

    yl, yr = moved(yhi, "gy", 1), moved(ylo, "gy", -1)
    xl, xr = moved(xhi, "gx", 1), moved(xlo, "gx", -1)
    clo, chi = pl.pallas_call(
        corner_kernel,
        out_shape=(tiles_of(C_TILES),) * 2,
        in_specs=[spec()] * 2,
        out_specs=[spec()] * 2,
        cost_estimate=estimate(0, 1 << 20),
        name="corners",
    )(yl, yr)
    cl, cr = moved(chi, "gx", 1), moved(clo, "gx", -1)

    weight_row = jnp.tile(spatial_weight, 2)[None, :]
    offset_rows = jnp.tile(orient_offsets.T, (1, 2))
    w_hi, w_lo, par = pl.pallas_call(
        weights_kernel,
        out_shape=(
            jax.ShapeDtypeStruct((256, 256), BF16),
            jax.ShapeDtypeStruct((256, 256), BF16),
            tiles_of(3),
        ),
        in_specs=[spec()] * 4,
        out_specs=[spec()] * 3,
        scratch_shapes=[pltpu.VMEM((128, 256), F32)],
        cost_estimate=estimate(4 << 20, 1 << 19),
        name="weights",
    )(dictionary, angular_weight, angular_weight.T, weight_row)

    own = jax.ShapeDtypeStruct((WX, WY, 8, 128), F32)
    frame = pltpu.VMEM((FX, FY, 8, 128), F32)
    as_tiles = lambda a: a.reshape(-1, 8, 128)
    as_field = lambda a: a.reshape(WX, WY, 8, 128)
    outs = pl.pallas_call(
        krylov_kernel,
        out_shape=(own,) * 7 + (jax.ShapeDtypeStruct((16, 128), F32),),
        in_specs=[spec(pl.ANY)] * 9 + [spec()] * 4,
        out_specs=[spec(pl.ANY)] * 7 + [spec()],
        scratch_shapes=[frame] * 9
        + [
            pltpu.VMEM((FX * FY * 8, 128), F32),
            frame,
            frame,
            pltpu.VMEM((12, 8, 128), F32),
            pltpu.VMEM((FX * FY, 128), F32),
            pltpu.SemaphoreType.DMA,
            pltpu.SemaphoreType.DMA,
        ],
        compiler_params=pltpu.CompilerParams(vmem_limit_bytes=40 << 20),
        cost_estimate=estimate(8 << 30, 8 << 20),
        name="krylov",
    )(
        as_field(dc), as_field(rc), as_tiles(mrow), as_tiles(yl), as_tiles(yr),
        as_tiles(xl), as_tiles(xr), as_tiles(cl), as_tiles(cr), w_hi, w_lo, par, offset_rows,
    )
    basis, part = outs[:7], outs[7]

    first = total_over(part, "gy")
    sums = lax.all_to_all(jnp.broadcast_to(first, (16, 128)), "gx", 0, 0, tiled=True)
    coef, flag = pl.pallas_call(
        scalars_kernel,
        out_shape=(
            jax.ShapeDtypeStruct((25, 8, 128), F32),
            jax.ShapeDtypeStruct((8, 128), jnp.int32),
        ),
        in_specs=[spec()] * 2,
        out_specs=[spec()] * 2,
        name="scalars",
    )(sums, par)

    def from_basis():
        return tuple(
            pl.pallas_call(
                combine_kernel,
                out_shape=(jax.ShapeDtypeStruct(iterate.shape, F32),) * 3,
                in_specs=[spec()] * 11,
                out_specs=[spec()] * 3,
                name="combine",
            )(iterate, dc, rc, *[b.reshape(-1, 128) for b in basis], coef)
        )

    def from_start():
        return plain_recurrence(
            iterate, residual, direction, brain_mask, dictionary, spatial_weight,
            angular_weight, orient_offsets,
        )

    return lax.cond(flag[0, 0] == 1, from_basis, from_start)


def solution(mesh):
    field = P("gx", "gy", None)
    in_specs = (field,) * 4 + (P(),) * 4
    return jax.shard_map(
        per_device, mesh=mesh, in_specs=in_specs, out_specs=(field,) * 3, check_vma=False
    )
```

```python
import functools

import jax
import jax.numpy as jnp
from jax import lax
from jax.experimental import pallas as pl
from jax.experimental.pallas import tpu as pltpu
from jax.sharding import PartitionSpec as P

ITERS = 4
AXES = ("gx", "gy")
AMPLIFICATION_LIMIT = 200.0
F32 = jnp.float32
BF16 = jnp.bfloat16

DIRECTIONS = [
    (0, 0, 1),
    (0, 1, -1),
    (0, 1, 0),
    (0, 1, 1),
    (1, -1, -1),
    (1, -1, 0),
    (1, -1, 1),
    (1, 0, -1),
    (1, 0, 0),
    (1, 0, 1),
    (1, 1, -1),
    (1, 1, 0),
    (1, 1, 1),
]

WX, WY = 8, 16
DEEP = 4
FX, FY = WX + 2 * DEEP, WY + 2 * DEEP
Y_TILES = WX * (DEEP + DEEP - 1) + 1
X_TILES = WY * (DEEP + DEEP - 1) + 2
C_TILES = DEEP * DEEP + (DEEP - 1) * (DEEP - 1) + 1
MOMENTS = 24


def padded_2(cells, sides, width):
    for axis, dim in sides:
        count = lax.axis_size(axis)
        ends = count - 1
        head = lax.slice_in_dim(cells, 0, width, axis=dim)
        tail = lax.slice_in_dim(cells, cells.shape[dim] - width, cells.shape[dim], axis=dim)
        cells = jnp.concatenate(
            [
                lax.ppermute(tail, axis, [(i, (i + 1) % count) for i in range(ends)]),
                cells,
                lax.ppermute(head, axis, [((i + 1) % count, i) for i in range(ends)]),
            ],
            axis=dim,
        )
    return cells


def angular_matrix(angular_weight):
    symmetric = 0.5 * (angular_weight + angular_weight.T)
    channels = symmetric.shape[0]
    coupling = symmetric * (1.0 - jnp.eye(channels, dtype=jnp.float32))
    return jnp.diag(jnp.sum(coupling, axis=1)) - coupling


def channel_selector(orient_offsets):
    table = jnp.array(DIRECTIONS, dtype=jnp.int32)
    hits = jnp.all(orient_offsets[None, :, :] == table[:, None, :], axis=-1)
    return hits.astype(jnp.float32)


def neighbour_sum(extended, selector, width_x, width_y, depth, channels):
    padded = jnp.pad(extended, ((0, 0), (0, 0), (channels, channels)))
    running_sum = jnp.zeros((width_x, width_y, depth), jnp.float32)
    slices = depth // channels
    for number in range(len(DIRECTIONS)):
        step_x, step_y, step_z = DIRECTIONS[number]
        forward = padded[
            1 + step_x : 1 + step_x + width_x,
            1 + step_y : 1 + step_y + width_y,
            channels + step_z * channels : channels + step_z * channels + depth,
        ]
        backward = padded[
            1 - step_x : 1 - step_x + width_x,
            1 - step_y : 1 - step_y + width_y,
            channels - step_z * channels : channels - step_z * channels + depth,
        ]
        running_sum = running_sum + jnp.tile(selector[number], slices) * (forward + backward)
    return running_sum


def apply_operator(field_data, brain_mask, dictionary, spatial_rows, angular_full, selector):
    extended = padded_2(field_data, (("gx", 0), ("gy", 1)), 1)
    width_x, width_y, depth = field_data.shape
    channels = dictionary.shape[1]
    flattened = field_data.reshape(-1, channels)
    dot = functools.partial(
        jnp.dot, precision=lax.Precision.HIGHEST, preferred_element_type=jnp.float32
    )
    back_proj = dot(dot(flattened, dictionary.T), dictionary)
    mask_rows = brain_mask.reshape(-1).astype(jnp.float32)
    data_term = (back_proj * mask_rows[:, None]).reshape(width_x, width_y, depth)
    angular_term = dot(flattened, angular_full).reshape(width_x, width_y, depth)
    neighbours = neighbour_sum(extended, selector, width_x, width_y, depth, channels)
    return data_term + angular_term + spatial_rows * (2.0 * field_data - neighbours)


def plain_recurrence(
    iterate, residual, direction, brain_mask, dictionary, spatial_weight, angular_weight, offsets
):
    angular_full = angular_matrix(angular_weight)
    selector = channel_selector(offsets)
    spatial_rows = jnp.tile(spatial_weight, iterate.shape[2] // dictionary.shape[1])

    def step(_, state):
        iterate, residual, direction, norm_now = state
        images = apply_operator(
            direction, brain_mask, dictionary, spatial_rows, angular_full, selector
        )
        curvature = lax.psum(jnp.sum(direction * images), AXES)
        step_length = norm_now / curvature
        iterate = iterate + step_length * direction
        residual = residual - step_length * images
        norm_next = lax.psum(jnp.sum(residual * residual), AXES)
        direction = residual + norm_next / norm_now * direction
        return iterate, residual, direction, norm_next

    norm = lax.psum(jnp.sum(residual * residual), AXES)
    state = lax.fori_loop(0, ITERS, step, (iterate, residual, direction, norm))
    return state[:3]


def pack_kernel(d_ref, r_ref, m_ref, dc, rc, mrow, ylo, yhi, xlo, xhi, cll, clh, chl, chh):
    for src, dst in ((d_ref, dc), (r_ref, rc)):
        for x in range(WX):
            for half in range(2):
                for k in range(8):
                    tile = src[x, 8 * half : 8 * half + 8, 128 * k : 128 * k + 128]
                    dst[pl.ds((x * WY + 8 * half) * 8 + k, 8, stride=8), :] = tile
    for y in range(WY):
        lane = 16 * (y % 8)
        mrow[8 * (y // 8) : 8 * (y // 8) + 8, lane : lane + 16] = m_ref[:, y, :].astype(F32)
    base = 8 * WX * DEEP
    for x in range(WX):
        row = x * WY * 8
        for src, wide, at in ((dc, DEEP, 0), (rc, DEEP - 1, base)):
            n = 8 * wide
            ylo[at + x * n : at + x * n + n, :] = src[row : row + n, :]
            yhi[at + x * n : at + x * n + n, :] = src[row + WY * 8 - n : row + WY * 8, :]
    last = 8 * (Y_TILES - 1)
    ylo[last:, :] = mrow[0:8, :]
    yhi[last:, :] = mrow[8:16, :]
    at = 0
    for src, wide in ((dc, DEEP), (rc, DEEP - 1)):
        n = 8 * WY * wide
        xlo[at : at + n, :] = src[0:n, :]
        xhi[at : at + n, :] = src[8 * WX * WY - n :, :]
        at += n
    xlo[at:, :] = mrow[...]
    xhi[at:, :] = mrow[...]
    at = 0
    for src, wide in ((dc, DEEP), (rc, DEEP - 1)):
        n = 8 * wide
        for i in range(wide):
            for low, high, x in ((cll, clh, i), (chl, chh, WX - wide + i)):
                row = x * WY * 8
                low[at : at + n, :] = src[row : row + n, :]
                high[at : at + n, :] = src[row + WY * 8 - n : row + WY * 8, :]
            at += n
    for low, high in ((cll, clh), (chl, chh)):
        low[at:, :] = mrow[0:8, :]
        high[at:, :] = mrow[8:16, :]


def weights_kernel(dict_ref, ang_ref, angt_ref, sw_ref, w_hi, w_lo, par, wide):
    dictionary = dict_ref[...]
    gram = lax.dot_general(
        dictionary,
        dictionary,
        (((0,), (0,)), ((), ())),
        precision=lax.Precision.HIGHEST,
        preferred_element_type=F32,
    )
    row = lax.broadcasted_iota(jnp.int32, (64, 64), 0)
    col = lax.broadcasted_iota(jnp.int32, (64, 64), 1)
    same = row == col
    coupling = jnp.where(same, 0.0, 0.5 * (ang_ref[...] + angt_ref[...]))
    degree = jnp.sum(coupling, axis=0, keepdims=True)
    weight = sw_ref[:, 0:64]
    angular = jnp.where(same, degree, 0.0) - coupling
    size = jnp.sum(jnp.abs(gram), axis=0, keepdims=True) + 2.0 * degree + 4.0 * weight
    scale = jnp.max(size, axis=1, keepdims=True)
    centre = jnp.sum(jnp.where(same, gram, 0.0), axis=0, keepdims=True) + degree + 2.0 * weight
    shift = jnp.sum(centre, axis=1, keepdims=True) * (1.0 / 64.0)
    inverse = 1.0 / scale
    first = gram * inverse
    second = (angular + jnp.where(same, 2.0 * weight - shift, 0.0)) * inverse
    wide[...] = jnp.zeros_like(wide)
    for half in range(2):
        at = 64 * half
        wide[at : at + 64, at : at + 64] = first
        wide[at : at + 64, 128 + at : 128 + at + 64] = second
    full = wide[...]
    high = full.astype(BF16)
    low = (full - high.astype(F32)).astype(BF16)
    w_hi[0:128, :] = high
    w_hi[128:256, :] = high
    w_lo[0:128, :] = low
    w_lo[128:256, :] = low
    par[0:8, :] = jnp.broadcast_to(sw_ref[...] * inverse, (8, 128))
    par[8:16, :] = jnp.broadcast_to(scale, (8, 128))
    par[16:24, :] = jnp.broadcast_to(shift, (8, 128))


def krylov_kernel(
    dc, rc, mrow, yl, yr, xl, xr, cll, clr, crl, crr, w_hi, w_lo, par, off,
    d1o, d2o, d3o, d4o, r1o, r2o, r3o, part,
    d0, d1, d2, d3, d4, r0, r1, r2, r3, me, qf, qb, tiles, lhs, out_sem,
):
    own_x, own_y = pl.ds(DEEP, WX), pl.ds(DEEP, WY)
    d0[own_x, own_y] = dc[...]
    r0[own_x, own_y] = rc[...]
    for wide, field, base, xbase, cbase in (
        (DEEP, d0, 0, 0, 0),
        (DEEP - 1, r0, WX * DEEP, WY * DEEP, DEEP * DEEP),
    ):
        lo, hi_y, hi_x = DEEP - wide, DEEP + WY, DEEP + WX
        for x in range(WX):
            at = base + wide * x
            field[DEEP + x, lo : lo + wide] = yl[at : at + wide]
            field[DEEP + x, hi_y : hi_y + wide] = yr[at : at + wide]
        for i in range(wide):
            for block, left, right, x in ((xl, cll, clr, lo + i), (xr, crl, crr, hi_x + i)):
                field[x, own_y] = block[xbase + WY * i : xbase + WY * i + WY]
                at = cbase + wide * i
                field[x, lo : lo + wide] = left[at : at + wide]
                field[x, hi_y : hi_y + wide] = right[at : at + wide]
    tiles[0] = yl[Y_TILES - 1]
    tiles[1:3] = mrow[...]
    tiles[3] = yr[Y_TILES - 1]
    for at, block, left, right in ((4, xl, cll, clr), (8, xr, crl, crr)):
        tiles[at] = left[C_TILES - 1]
        tiles[at + 1 : at + 3] = block[X_TILES - 2 : X_TILES]
        tiles[at + 3] = right[C_TILES - 1]

    sub = lax.broadcasted_iota(jnp.int32, (8, 128), 0)
    lane = lax.broadcasted_iota(jnp.int32, (8, 128), 1)
    off_x = jnp.broadcast_to(off[0:1, :], (8, 128))
    off_y = jnp.broadcast_to(off[1:2, :], (8, 128))
    off_z = jnp.broadcast_to(off[2:3, :], (8, 128))
    lower = lane < 64
    flat_z = off_z == 0
    direct = jnp.logical_or(
        jnp.logical_and(lower, off_z == 1), jnp.logical_and(lane >= 64, off_z == -1)
    )
    edge = jnp.logical_or(
        jnp.logical_and(lower, sub == 0), jnp.logical_and(lane >= 64, sub == 7)
    )
    inside = jnp.where(edge, 0.0, 1.0).astype(F32)
    y_minus, y_plus, x_step = off_y == -1, off_y == 1, off_x == 1
    weight = par[0:8, :]

    for frame_y in range(1, FY - 1):
        y = frame_y - DEEP + 8
        group, amount = y // 8, 16 * (y % 8)
        column = jnp.concatenate(
            [tiles[4 + group][4:8], tiles[group], tiles[8 + group][0:4]], axis=0
        )
        if amount:
            column = pltpu.roll(column, 128 - amount, 1)
        lhs[pl.ds(frame_y, FX, stride=FY), :] = column
    slots = lhs[...].astype(BF16)
    z_row = lax.broadcasted_iota(jnp.int32, (128, 128), 0)
    z_lane = lax.broadcasted_iota(jnp.int32, (128, 128), 1) // 64
    for k in range(8):
        spread = jnp.where(z_row == 2 * k + z_lane, 1.0, 0.0).astype(BF16)
        me[pl.ds(k, FX * FY, stride=8), :] = jnp.dot(
            slots, spread, preferred_element_type=F32
        )

    gx, gy = lax.axis_index("gx"), lax.axis_index("gy")
    ends_x, ends_y = lax.axis_size("gx") - 1, lax.axis_size("gy") - 1

    def operator(src, dst, depth):
        lo, wide = DEEP - depth, WY + 2 * depth
        inner = wide - 2

        def shift_row(x, _):
            v = src[x, pl.ds(lo, wide)]
            rot = pltpu.roll(v, 64, 2)
            far = jnp.where(lower, pltpu.roll(rot, 1, 1), pltpu.roll(rot, 7, 1)) * inside
            u = jnp.where(flat_z, v, jnp.where(direct, rot, far))
            w = jnp.where(flat_z, v, jnp.where(direct, far, rot))
            qf[x, pl.ds(lo + 1, inner)] = jnp.where(
                y_minus, u[:-2], jnp.where(y_plus, u[2:], u[1:-1])
            )
            qb[x, pl.ds(lo + 1, inner)] = jnp.where(
                y_minus, w[2:], jnp.where(y_plus, w[:-2], w[1:-1])
            )
            return 0

        lax.fori_loop(lo, FX - lo, shift_row, 0)

        def combine_row(x, _):
            cols = pl.ds(lo + 1, inner)
            v = src[x, cols].reshape(inner * 8, 128)
            high = v.astype(BF16)
            low = (v - high.astype(F32)).astype(BF16)
            both = jnp.concatenate([high, low], axis=1)
            prod = jnp.dot(both, w_hi[...], preferred_element_type=F32)
            prod = prod + jnp.dot(both, w_lo[...], preferred_element_type=F32)
            near = jnp.where(x_step, qf[x + 1, cols], qf[x, cols])
            near = near + jnp.where(x_step, qb[x - 1, cols], qb[x, cols])
            data = prod[:, 0:128].reshape(inner, 8, 128)
            rest = prod[:, 128:256].reshape(inner, 8, 128)
            start = pl.multiple_of((x * FY + lo + 1) * 8, 8)
            mask = me[pl.ds(start, inner * 8), :].reshape(inner, 8, 128)
            dst[x, cols] = mask * data + rest - weight * near
            return 0

        lax.fori_loop(lo + 1, FX - lo - 1, combine_row, 0)

        border = depth - 1
        if border:
            zero_rows = jnp.zeros((border, inner, 8, 128), F32)
            zero_cols = jnp.zeros((WX + 2 * border, border, 8, 128), F32)
            rows, cols = pl.ds(lo + 1, FX - 2 * lo - 2), pl.ds(lo + 1, inner)

            @pl.when(gx == 0)
            def _():
                dst[pl.ds(lo + 1, border), cols] = zero_rows

            @pl.when(gx == ends_x)
            def _():
                dst[pl.ds(DEEP + WX, border), cols] = zero_rows

            @pl.when(gy == 0)
            def _():
                dst[rows, pl.ds(lo + 1, border)] = zero_cols

            @pl.when(gy == ends_y)
            def _():
                dst[rows, pl.ds(DEEP + WY, border)] = zero_cols

    stores = []

    def put(src, dst):
        copy = pltpu.make_async_copy(src.at[own_x, own_y], dst, out_sem)
        copy.start()
        stores.append(copy)

    for src, dst, out, depth in (
        (d0, d1, d1o, 4),
        (d1, d2, d2o, 3),
        (r0, r1, r1o, 3),
        (d2, d3, d3o, 2),
        (r1, r2, r2o, 2),
        (d3, d4, d4o, 1),
        (r2, r3, r3o, 1),
    ):
        operator(src, dst, depth)
        put(dst, out)

    ds, rs = (d0, d1, d2, d3, d4), (r0, r1, r2, r3)
    pairs = [(ds[k // 2], ds[k - k // 2]) for k in range(9)]
    pairs += [(rs[min(k // 2, 3)], ds[k - min(k // 2, 3)]) for k in range(8)]
    pairs += [(rs[k // 2], rs[k - k // 2]) for k in range(7)]

    def accumulate(i, acc):
        x, y = DEEP + i // 2, DEEP + 8 * (i % 2)
        cols = pl.ds(y, 8)
        loaded = {id(f): f[x, cols] for f in ds + rs}
        return tuple(
            a + jnp.sum(loaded[id(f)] * loaded[id(g)], axis=0)
            for a, (f, g) in zip(acc, pairs)
        )

    zero = jnp.zeros((8, 128), F32)
    acc = lax.fori_loop(0, 2 * WX, accumulate, (zero,) * MOMENTS)
    total = zero[0:1, :]
    lane_row = lax.broadcasted_iota(jnp.int32, (1, 128), 1)
    for k, a in enumerate(acc):
        value = jnp.sum(jnp.sum(a, axis=0, keepdims=True), axis=1, keepdims=True)
        total = jnp.where(lane_row == k, value, total)
    part[...] = jnp.broadcast_to(total, part.shape)
    for copy in stores:
        copy.wait()


def scalars_kernel(sums, par, coef, flag):
    row = jnp.sum(sums[...], axis=0, keepdims=True)
    moment = [jnp.broadcast_to(row[:, k : k + 1], (8, 128)) for k in range(MOMENTS)]
    mu, nu, rho = moment[0:9], moment[9:17], moment[17:24]
    scale = par[8:16, :]
    inverse = 1.0 / scale
    sigma = par[16:24, :] * inverse
    one, zero = jnp.ones((8, 128), F32), jnp.zeros((8, 128), F32)

    def product(p, q):
        out = [None] * max(len(p) + len(q) - 1, 0)
        for i, a in enumerate(p):
            for j, b in enumerate(q):
                out[i + j] = a * b if out[i + j] is None else out[i + j] + a * b
        return out

    def form(v, w):
        crossed = product(v[0], w[1]), product(w[0], v[1])
        total, size = zero, zero
        for c, m in ((product(v[0], w[0]), mu), (product(v[1], w[1]), rho)):
            for a, b in zip(c, m):
                total, size = total + a * b, size + jnp.abs(a * b)
        for a, b, m in zip(crossed[0], crossed[1], nu):
            total, size = total + (a + b) * m, size + (jnp.abs(a) + jnp.abs(b)) * jnp.abs(m)
        return total, size

    def add(p, factor, q):
        out = []
        for i in range(max(len(p), len(q))):
            if i >= len(q):
                out.append(p[i])
            elif i >= len(p):
                out.append(factor * q[i])
            else:
                out.append(p[i] + factor * q[i])
        return out

    def image(v):
        return tuple(add([zero] + p, sigma, p) if p else [] for p in v)

    xs, rs, ds = ([], []), ([], [one]), ([one], [])
    norm = rho[0]
    worst = zero
    for _ in range(ITERS):
        applied = image(ds)
        curvature, size = form(ds, applied)
        worst = jnp.maximum(worst, size / jnp.abs(curvature))
        bad = jnp.logical_not(size <= AMPLIFICATION_LIMIT * curvature)
        step = norm / curvature
        xs = tuple(add(p, step, q) for p, q in zip(xs, ds))
        rs = tuple(add(p, -step, q) for p, q in zip(rs, applied))
        after, size = form(rs, rs)
        bad = jnp.logical_or(bad, jnp.logical_not(size <= AMPLIFICATION_LIMIT * after))
        worst = jnp.where(bad, 2.0 * AMPLIFICATION_LIMIT, worst)
        ds = tuple(add(p, after / norm, q) for p, q in zip(rs, ds))
        norm = after
    rows = [a * inverse for a in xs[0] + xs[1]] + rs[0] + rs[1] + ds[0] + ds[1]
    for k, a in enumerate(rows):
        coef[k] = a
    flag[0] = jnp.where(jnp.max(worst) <= AMPLIFICATION_LIMIT, 1, 0).astype(jnp.int32)


def combine_kernel(x_ref, dc, rc, d1, d2, d3, d4, r1, r2, r3, coef, xo, ro, do):
    c = [coef[k] for k in range(25)]
    fields = (dc, d1, d2, d3, d4, rc, r1, r2, r3)
    to_x = dict(zip((0, 1, 2, 3, 5, 6, 7), c[0:7]))

    def row(x, _):
        for half in range(2):
            for k in range(8):
                at = (x * WY + 8 * half) * 8 + k
                b = [f[pl.ds(at, 8, stride=8), :] for f in fields]
                place = (x, slice(8 * half, 8 * half + 8), slice(128 * k, 128 * k + 128))
                value = x_ref[place]
                for i, a in to_x.items():
                    value = value + a * b[i]
                xo[place] = value
                for out, base in ((ro, 7), (do, 16)):
                    value = c[base] * b[0]
                    for i in range(1, 9):
                        value = value + c[base + i] * b[i]
                    out[place] = value
        return 0

    lax.fori_loop(0, WX, row, 0)


def spec(space=pltpu.VMEM):
    return pl.BlockSpec(memory_space=space)


def tiles_of(n):
    return jax.ShapeDtypeStruct((n * 8, 128), F32)


def estimate(flops, bytes_accessed):
    return pl.CostEstimate(flops=flops, bytes_accessed=bytes_accessed, transcendentals=0)


def moved(value, axis, step):
    count = lax.axis_size(axis)
    pairs = [(i, i + step) for i in range(count) if 0 <= i + step < count]
    return lax.ppermute(value, axis, pairs)


def moved_across(value, step_x, step_y):
    count_x, count_y = lax.axis_size("gx"), lax.axis_size("gy")
    pairs = [
        (x * count_y + y, (x + step_x) * count_y + y + step_y)
        for x in range(count_x)
        for y in range(count_y)
        if 0 <= x + step_x < count_x and 0 <= y + step_y < count_y
    ]
    return lax.ppermute(value, AXES, pairs)


def total_over(rows, axis):
    return jnp.sum(lax.all_to_all(rows, axis, 0, 0, tiled=True), axis=0, keepdims=True)


def per_device(
    iterate,
    residual,
    direction,
    brain_mask,
    dictionary,
    spatial_weight,
    angular_weight,
    orient_offsets,
):
    cells = WX * WY
    dc, rc, mrow, ylo, yhi, xlo, xhi, cll, clh, chl, chh = pl.pallas_call(
        pack_kernel,
        out_shape=(
            tiles_of(cells), tiles_of(cells), tiles_of(2), tiles_of(Y_TILES),
            tiles_of(Y_TILES), tiles_of(X_TILES), tiles_of(X_TILES),
        )
        + (tiles_of(C_TILES),) * 4,
        in_specs=[spec()] * 3,
        out_specs=[spec()] * 11,
        cost_estimate=estimate(0, 4 << 20),
        name="pack",
    )(direction, residual, brain_mask)

    yl, yr = moved(yhi, "gy", 1), moved(ylo, "gy", -1)
    xl, xr = moved(xhi, "gx", 1), moved(xlo, "gx", -1)
    from_ll, from_lh = moved_across(chh, 1, 1), moved_across(chl, 1, -1)
    from_hl, from_hh = moved_across(clh, -1, 1), moved_across(cll, -1, -1)

    weight_row = jnp.tile(spatial_weight, 2)[None, :]
    offset_rows = jnp.tile(orient_offsets.T, (1, 2))
    w_hi, w_lo, par = pl.pallas_call(
        weights_kernel,
        out_shape=(
            jax.ShapeDtypeStruct((256, 256), BF16),
            jax.ShapeDtypeStruct((256, 256), BF16),
            tiles_of(3),
        ),
        in_specs=[spec()] * 4,
        out_specs=[spec()] * 3,
        scratch_shapes=[pltpu.VMEM((128, 256), F32)],
        cost_estimate=estimate(4 << 20, 1 << 19),
        name="weights",
    )(dictionary, angular_weight, angular_weight.T, weight_row)

    own = jax.ShapeDtypeStruct((WX, WY, 8, 128), F32)
    frame = pltpu.VMEM((FX, FY, 8, 128), F32)
    as_tiles = lambda a: a.reshape(-1, 8, 128)
    as_field = lambda a: a.reshape(WX, WY, 8, 128)
    outs = pl.pallas_call(
        krylov_kernel,
        out_shape=(own,) * 7 + (jax.ShapeDtypeStruct((16, 128), F32),),
        in_specs=[spec()] * 15,
        out_specs=[spec(pl.ANY)] * 7 + [spec()],
        scratch_shapes=[frame] * 9
        + [
            pltpu.VMEM((FX * FY * 8, 128), F32),
            frame,
            frame,
            pltpu.VMEM((12, 8, 128), F32),
            pltpu.VMEM((FX * FY, 128), F32),
            pltpu.SemaphoreType.DMA,
        ],
        compiler_params=pltpu.CompilerParams(vmem_limit_bytes=40 << 20),
        cost_estimate=estimate(8 << 30, 8 << 20),
        name="krylov",
    )(
        as_field(dc), as_field(rc), as_tiles(mrow), as_tiles(yl), as_tiles(yr),
        as_tiles(xl), as_tiles(xr), as_tiles(from_ll), as_tiles(from_lh), as_tiles(from_hl),
        as_tiles(from_hh), w_hi, w_lo, par, offset_rows,
    )
    basis, part = outs[:7], outs[7]

    first = total_over(part, "gy")
    sums = lax.all_to_all(jnp.broadcast_to(first, (16, 128)), "gx", 0, 0, tiled=True)
    coef, flag = pl.pallas_call(
        scalars_kernel,
        out_shape=(
            jax.ShapeDtypeStruct((25, 8, 128), F32),
            jax.ShapeDtypeStruct((1,), jnp.int32),
        ),
        in_specs=[spec()] * 2,
        out_specs=[spec(), spec(pltpu.SMEM)],
        name="scalars",
    )(sums, par)

    def from_basis():
        return tuple(
            pl.pallas_call(
                combine_kernel,
                out_shape=(jax.ShapeDtypeStruct(iterate.shape, F32),) * 3,
                in_specs=[spec()] * 11,
                out_specs=[spec()] * 3,
                name="combine",
            )(iterate, dc, rc, *[b.reshape(-1, 128) for b in basis], coef)
        )

    def from_start():
        return plain_recurrence(
            iterate, residual, direction, brain_mask, dictionary, spatial_weight,
            angular_weight, orient_offsets,
        )

    return lax.cond(flag[0] == 1, from_basis, from_start)


def solution(mesh):
    field = P("gx", "gy", None)
    in_specs = (field,) * 4 + (P(),) * 4
    return jax.shard_map(
        per_device, mesh=mesh, in_specs=in_specs, out_specs=(field,) * 3, check_vma=False
    )
```

```python
import functools

import jax
import jax.numpy as jnp
from jax import lax
from jax.experimental import pallas as pl
from jax.experimental.pallas import tpu as pltpu
from jax.sharding import PartitionSpec as P

ITERS = 4
AXES = ("gx", "gy")
AMPLIFICATION_LIMIT = 200.0
F32 = jnp.float32
BF16 = jnp.bfloat16

DIRECTIONS = [
    (0, 0, 1),
    (0, 1, -1),
    (0, 1, 0),
    (0, 1, 1),
    (1, -1, -1),
    (1, -1, 0),
    (1, -1, 1),
    (1, 0, -1),
    (1, 0, 0),
    (1, 0, 1),
    (1, 1, -1),
    (1, 1, 0),
    (1, 1, 1),
]

WX, WY = 8, 16
DEEP = 4
FX, FY = WX + 2 * DEEP, WY + 2 * DEEP
Y_TILES = WX * (DEEP + DEEP - 1) + 1
X_TILES = WY * (DEEP + DEEP - 1) + 2
C_TILES = DEEP * DEEP + (DEEP - 1) * (DEEP - 1) + 1
ROW_TILES = X_TILES + 2 * C_TILES
MOMENTS = 24


def padded_2(cells, sides, width):
    for axis, dim in sides:
        count = lax.axis_size(axis)
        ends = count - 1
        head = lax.slice_in_dim(cells, 0, width, axis=dim)
        tail = lax.slice_in_dim(cells, cells.shape[dim] - width, cells.shape[dim], axis=dim)
        cells = jnp.concatenate(
            [
                lax.ppermute(tail, axis, [(i, (i + 1) % count) for i in range(ends)]),
                cells,
                lax.ppermute(head, axis, [((i + 1) % count, i) for i in range(ends)]),
            ],
            axis=dim,
        )
    return cells


def angular_matrix(angular_weight):
    symmetric = 0.5 * (angular_weight + angular_weight.T)
    channels = symmetric.shape[0]
    coupling = symmetric * (1.0 - jnp.eye(channels, dtype=jnp.float32))
    return jnp.diag(jnp.sum(coupling, axis=1)) - coupling


def channel_selector(orient_offsets):
    table = jnp.array(DIRECTIONS, dtype=jnp.int32)
    hits = jnp.all(orient_offsets[None, :, :] == table[:, None, :], axis=-1)
    return hits.astype(jnp.float32)


def neighbour_sum(extended, selector, width_x, width_y, depth, channels):
    padded = jnp.pad(extended, ((0, 0), (0, 0), (channels, channels)))
    running_sum = jnp.zeros((width_x, width_y, depth), jnp.float32)
    slices = depth // channels
    for number in range(len(DIRECTIONS)):
        step_x, step_y, step_z = DIRECTIONS[number]
        forward = padded[
            1 + step_x : 1 + step_x + width_x,
            1 + step_y : 1 + step_y + width_y,
            channels + step_z * channels : channels + step_z * channels + depth,
        ]
        backward = padded[
            1 - step_x : 1 - step_x + width_x,
            1 - step_y : 1 - step_y + width_y,
            channels - step_z * channels : channels - step_z * channels + depth,
        ]
        running_sum = running_sum + jnp.tile(selector[number], slices) * (forward + backward)
    return running_sum


def apply_operator(field_data, brain_mask, dictionary, spatial_rows, angular_full, selector):
    extended = padded_2(field_data, (("gx", 0), ("gy", 1)), 1)
    width_x, width_y, depth = field_data.shape
    channels = dictionary.shape[1]
    flattened = field_data.reshape(-1, channels)
    dot = functools.partial(
        jnp.dot, precision=lax.Precision.HIGHEST, preferred_element_type=jnp.float32
    )
    back_proj = dot(dot(flattened, dictionary.T), dictionary)
    mask_rows = brain_mask.reshape(-1).astype(jnp.float32)
    data_term = (back_proj * mask_rows[:, None]).reshape(width_x, width_y, depth)
    angular_term = dot(flattened, angular_full).reshape(width_x, width_y, depth)
    neighbours = neighbour_sum(extended, selector, width_x, width_y, depth, channels)
    return data_term + angular_term + spatial_rows * (2.0 * field_data - neighbours)


def plain_recurrence(
    iterate, residual, direction, brain_mask, dictionary, spatial_weight, angular_weight, offsets
):
    angular_full = angular_matrix(angular_weight)
    selector = channel_selector(offsets)
    spatial_rows = jnp.tile(spatial_weight, iterate.shape[2] // dictionary.shape[1])

    def step(_, state):
        iterate, residual, direction, norm_now = state
        images = apply_operator(
            direction, brain_mask, dictionary, spatial_rows, angular_full, selector
        )
        curvature = lax.psum(jnp.sum(direction * images), AXES)
        step_length = norm_now / curvature
        iterate = iterate + step_length * direction
        residual = residual - step_length * images
        norm_next = lax.psum(jnp.sum(residual * residual), AXES)
        direction = residual + norm_next / norm_now * direction
        return iterate, residual, direction, norm_next

    norm = lax.psum(jnp.sum(residual * residual), AXES)
    state = lax.fori_loop(0, ITERS, step, (iterate, residual, direction, norm))
    return state[:3]


def pack_kernel(d_ref, r_ref, m_ref, dc, rc, mrow, ylo, yhi, xlo, xhi):
    for src, dst in ((d_ref, dc), (r_ref, rc)):
        for x in range(WX):
            for half in range(2):
                for k in range(8):
                    tile = src[x, 8 * half : 8 * half + 8, 128 * k : 128 * k + 128]
                    dst[pl.ds((x * WY + 8 * half) * 8 + k, 8, stride=8), :] = tile
    for y in range(WY):
        lane = 16 * (y % 8)
        mrow[8 * (y // 8) : 8 * (y // 8) + 8, lane : lane + 16] = m_ref[:, y, :].astype(F32)
    base = 8 * WX * DEEP
    for x in range(WX):
        row = x * WY * 8
        for src, wide, at in ((dc, DEEP, 0), (rc, DEEP - 1, base)):
            n = 8 * wide
            ylo[at + x * n : at + x * n + n, :] = src[row : row + n, :]
            yhi[at + x * n : at + x * n + n, :] = src[row + WY * 8 - n : row + WY * 8, :]
    last = 8 * (Y_TILES - 1)
    ylo[last:, :] = mrow[0:8, :]
    yhi[last:, :] = mrow[8:16, :]
    at = 0
    for src, wide in ((dc, DEEP), (rc, DEEP - 1)):
        n = 8 * WY * wide
        xlo[at : at + n, :] = src[0:n, :]
        xhi[at : at + n, :] = src[8 * WX * WY - n :, :]
        at += n
    xlo[at : at + 16, :] = mrow[...]
    xhi[at : at + 16, :] = mrow[...]


def corner_kernel(left, right, low_in, high_in, xlo, xhi, sem):
    del low_in, high_in
    d, r = 8 * DEEP, 8 * (DEEP - 1)
    base = WX * d
    copies = []
    for out, d_from, r_from in ((xlo, 0, base), (xhi, (WX - DEEP) * d, base + (WX - DEEP + 1) * r)):
        at = 8 * X_TILES
        for side in (left, right):
            for start, rows in ((d_from, DEEP * d), (r_from, (DEEP - 1) * r), (8 * (Y_TILES - 1), 8)):
                copy = pltpu.make_async_copy(
                    side.at[pl.ds(start, rows)], out.at[pl.ds(at, rows)], sem
                )
                copy.start()
                copies.append(copy)
                at += rows
    for copy in copies:
        copy.wait()


def weights_kernel(dict_ref, ang_ref, angt_ref, sw_ref, wide):
    dictionary = dict_ref[...]
    gram = lax.dot_general(
        dictionary,
        dictionary,
        (((0,), (0,)), ((), ())),
        precision=lax.Precision.HIGHEST,
        preferred_element_type=F32,
    )
    row = lax.broadcasted_iota(jnp.int32, (64, 64), 0)
    col = lax.broadcasted_iota(jnp.int32, (64, 64), 1)
    same = row == col
    coupling = jnp.where(same, 0.0, 0.5 * (ang_ref[...] + angt_ref[...]))
    degree = jnp.sum(coupling, axis=0, keepdims=True)
    weight = sw_ref[:, 0:64]
    angular = jnp.where(same, degree, 0.0) - coupling
    size = jnp.sum(jnp.abs(gram), axis=0, keepdims=True) + 2.0 * degree + 4.0 * weight
    scale = jnp.max(size, axis=1, keepdims=True)
    centre = jnp.sum(jnp.where(same, gram, 0.0), axis=0, keepdims=True) + degree + 2.0 * weight
    shift = jnp.sum(centre, axis=1, keepdims=True) * (1.0 / 64.0)
    inverse = 1.0 / scale
    first = gram * inverse
    second = (angular + jnp.where(same, 2.0 * weight - shift, 0.0)) * inverse
    wide[...] = jnp.zeros_like(wide)
    for half in range(2):
        at = 64 * half
        wide[at : at + 64, at : at + 64] = first
        wide[at : at + 64, 128 + at : 128 + at + 64] = second
    wide[128:136, 0:128] = jnp.broadcast_to(sw_ref[...] * inverse, (8, 128))
    wide[136:144, 0:128] = jnp.broadcast_to(scale, (8, 128))
    wide[144:152, 0:128] = jnp.broadcast_to(shift, (8, 128))


def krylov_kernel(
    dc, rc, xl, xr, off, wide_in, yl_in, yr_in, mrow_in,
    d1o, d2o, d3o, d4o, r1o, r2o, r3o, part,
    d0, d1, d2, d3, d4, r0, r1, r2, r3, me, qf, qb, tiles, lhs, yl, yr, mrow, w_hi, w_lo, in_sem, out_sem,
):
    fetches = [
        pltpu.make_async_copy(src, dst, in_sem)
        for src, dst in ((yl_in, yl), (yr_in, yr), (mrow_in, mrow))
    ]
    for copy in fetches:
        copy.start()
    own_x, own_y = pl.ds(DEEP, WX), pl.ds(DEEP, WY)
    d0[own_x, own_y] = dc[...]
    r0[own_x, own_y] = rc[...]
    full = wide_in[0:128, :]
    high = full.astype(BF16)
    low = (full - high.astype(F32)).astype(BF16)
    w_hi[0:128, :] = high
    w_hi[128:256, :] = high
    w_lo[0:128, :] = low
    w_lo[128:256, :] = low
    for copy in fetches:
        copy.wait()
    for wide, field, base, xbase, cbase in (
        (DEEP, d0, 0, 0, X_TILES),
        (DEEP - 1, r0, WX * DEEP, WY * DEEP, X_TILES + DEEP * DEEP),
    ):
        lo, hi_y, hi_x = DEEP - wide, DEEP + WY, DEEP + WX
        for x in range(WX):
            at = base + wide * x
            field[DEEP + x, lo : lo + wide] = yl[at : at + wide]
            field[DEEP + x, hi_y : hi_y + wide] = yr[at : at + wide]
        for i in range(wide):
            for block, x in ((xl, lo + i), (xr, hi_x + i)):
                field[x, own_y] = block[xbase + WY * i : xbase + WY * i + WY]
                at = cbase + wide * i
                field[x, lo : lo + wide] = block[at : at + wide]
                at += C_TILES
                field[x, hi_y : hi_y + wide] = block[at : at + wide]
    tiles[0] = yl[Y_TILES - 1]
    tiles[1:3] = mrow[...]
    tiles[3] = yr[Y_TILES - 1]
    for at, block in ((4, xl), (8, xr)):
        tiles[at] = block[X_TILES + C_TILES - 1]
        tiles[at + 1 : at + 3] = block[X_TILES - 2 : X_TILES]
        tiles[at + 3] = block[ROW_TILES - 1]

    sub = lax.broadcasted_iota(jnp.int32, (8, 128), 0)
    lane = lax.broadcasted_iota(jnp.int32, (8, 128), 1)
    off_x = jnp.broadcast_to(off[0:1, :], (8, 128))
    off_y = jnp.broadcast_to(off[1:2, :], (8, 128))
    off_z = jnp.broadcast_to(off[2:3, :], (8, 128))
    lower = lane < 64
    flat_z = off_z == 0
    direct = jnp.logical_or(
        jnp.logical_and(lower, off_z == 1), jnp.logical_and(lane >= 64, off_z == -1)
    )
    edge = jnp.logical_or(
        jnp.logical_and(lower, sub == 0), jnp.logical_and(lane >= 64, sub == 7)
    )
    inside = jnp.where(edge, 0.0, 1.0).astype(F32)
    y_minus, y_plus, x_step = off_y == -1, off_y == 1, off_x == 1
    weight = wide_in[128:136, 0:128]

    for frame_y in range(1, FY - 1):
        y = frame_y - DEEP + 8
        group, amount = y // 8, 16 * (y % 8)
        column = jnp.concatenate(
            [tiles[4 + group][4:8], tiles[group], tiles[8 + group][0:4]], axis=0
        )
        if amount:
            column = pltpu.roll(column, 128 - amount, 1)
        lhs[pl.ds(frame_y, FX, stride=FY), :] = column
    slots = lhs[...].astype(BF16)
    z_row = lax.broadcasted_iota(jnp.int32, (128, 128), 0)
    z_lane = lax.broadcasted_iota(jnp.int32, (128, 128), 1) // 64
    for k in range(8):
        spread = jnp.where(z_row == 2 * k + z_lane, 1.0, 0.0).astype(BF16)
        me[pl.ds(k, FX * FY, stride=8), :] = jnp.dot(
            slots, spread, preferred_element_type=F32
        )

    gx, gy = lax.axis_index("gx"), lax.axis_index("gy")
    ends_x, ends_y = lax.axis_size("gx") - 1, lax.axis_size("gy") - 1

    def operator(src, dst, depth):
        lo, wide = DEEP - depth, WY + 2 * depth
        inner = wide - 2

        def shift_row(x, _):
            v = src[x, pl.ds(lo, wide)]
            rot = pltpu.roll(v, 64, 2)
            far = jnp.where(lower, pltpu.roll(rot, 1, 1), pltpu.roll(rot, 7, 1)) * inside
            u = jnp.where(flat_z, v, jnp.where(direct, rot, far))
            w = jnp.where(flat_z, v, jnp.where(direct, far, rot))
            qf[x, pl.ds(lo + 1, inner)] = jnp.where(
                y_minus, u[:-2], jnp.where(y_plus, u[2:], u[1:-1])
            )
            qb[x, pl.ds(lo + 1, inner)] = jnp.where(
                y_minus, w[2:], jnp.where(y_plus, w[:-2], w[1:-1])
            )
            return 0

        lax.fori_loop(lo, FX - lo, shift_row, 0)

        def combine_row(x, _):
            cols = pl.ds(lo + 1, inner)
            v = src[x, cols].reshape(inner * 8, 128)
            high = v.astype(BF16)
            low = (v - high.astype(F32)).astype(BF16)
            both = jnp.concatenate([high, low], axis=1)
            prod = jnp.dot(both, w_hi[...], preferred_element_type=F32)
            prod = prod + jnp.dot(both, w_lo[...], preferred_element_type=F32)
            near = jnp.where(x_step, qf[x + 1, cols], qf[x, cols])
            near = near + jnp.where(x_step, qb[x - 1, cols], qb[x, cols])
            data = prod[:, 0:128].reshape(inner, 8, 128)
            rest = prod[:, 128:256].reshape(inner, 8, 128)
            start = pl.multiple_of((x * FY + lo + 1) * 8, 8)
            mask = me[pl.ds(start, inner * 8), :].reshape(inner, 8, 128)
            dst[x, cols] = mask * data + rest - weight * near
            return 0

        lax.fori_loop(lo + 1, FX - lo - 1, combine_row, 0, unroll=2)

        border = depth - 1
        if border:
            zero_rows = jnp.zeros((border, inner, 8, 128), F32)
            zero_cols = jnp.zeros((WX + 2 * border, border, 8, 128), F32)
            rows, cols = pl.ds(lo + 1, FX - 2 * lo - 2), pl.ds(lo + 1, inner)

            @pl.when(gx == 0)
            def _():
                dst[pl.ds(lo + 1, border), cols] = zero_rows

            @pl.when(gx == ends_x)
            def _():
                dst[pl.ds(DEEP + WX, border), cols] = zero_rows

            @pl.when(gy == 0)
            def _():
                dst[rows, pl.ds(lo + 1, border)] = zero_cols

            @pl.when(gy == ends_y)
            def _():
                dst[rows, pl.ds(DEEP + WY, border)] = zero_cols

    stores = []

    def put(src, dst):
        copy = pltpu.make_async_copy(src.at[own_x, own_y], dst, out_sem)
        copy.start()
        stores.append(copy)

    for src, dst, out, depth in (
        (d0, d1, d1o, 4),
        (d1, d2, d2o, 3),
        (r0, r1, r1o, 3),
        (d2, d3, d3o, 2),
        (r1, r2, r2o, 2),
        (d3, d4, d4o, 1),
        (r2, r3, r3o, 1),
    ):
        operator(src, dst, depth)
        put(dst, out)

    ds, rs = (d0, d1, d2, d3, d4), (r0, r1, r2, r3)
    pairs = [(ds[k // 2], ds[k - k // 2]) for k in range(9)]
    pairs += [(rs[min(k // 2, 3)], ds[k - min(k // 2, 3)]) for k in range(8)]
    pairs += [(rs[k // 2], rs[k - k // 2]) for k in range(7)]

    def accumulate(i, acc):
        x, y = DEEP + i // 2, DEEP + 8 * (i % 2)
        cols = pl.ds(y, 8)
        loaded = {id(f): f[x, cols] for f in ds + rs}
        return tuple(
            a + jnp.sum(loaded[id(f)] * loaded[id(g)], axis=0)
            for a, (f, g) in zip(acc, pairs)
        )

    zero = jnp.zeros((8, 128), F32)
    acc = lax.fori_loop(0, 2 * WX, accumulate, (zero,) * MOMENTS)
    total = zero[0:1, :]
    lane_row = lax.broadcasted_iota(jnp.int32, (1, 128), 1)
    for k, a in enumerate(acc):
        value = jnp.sum(jnp.sum(a, axis=0, keepdims=True), axis=1, keepdims=True)
        total = jnp.where(lane_row == k, value, total)
    part[...] = jnp.broadcast_to(total, part.shape)
    for copy in stores:
        copy.wait()


def scalars_kernel(sums, par, coef, flag):
    row = jnp.sum(sums[...], axis=0, keepdims=True)
    moment = [jnp.broadcast_to(row[:, k : k + 1], (8, 128)) for k in range(MOMENTS)]
    mu, nu, rho = moment[0:9], moment[9:17], moment[17:24]
    scale = par[136:144, 0:128]
    inverse = 1.0 / scale
    sigma = par[144:152, 0:128] * inverse
    one, zero = jnp.ones((8, 128), F32), jnp.zeros((8, 128), F32)

    def product(p, q):
        out = [None] * max(len(p) + len(q) - 1, 0)
        for i, a in enumerate(p):
            for j, b in enumerate(q):
                out[i + j] = a * b if out[i + j] is None else out[i + j] + a * b
        return out

    def form(v, w):
        crossed = product(v[0], w[1]), product(w[0], v[1])
        total, size = zero, zero
        for c, m in ((product(v[0], w[0]), mu), (product(v[1], w[1]), rho)):
            for a, b in zip(c, m):
                total, size = total + a * b, size + jnp.abs(a * b)
        for a, b, m in zip(crossed[0], crossed[1], nu):
            total, size = total + (a + b) * m, size + (jnp.abs(a) + jnp.abs(b)) * jnp.abs(m)
        return total, size

    def add(p, factor, q):
        out = []
        for i in range(max(len(p), len(q))):
            if i >= len(q):
                out.append(p[i])
            elif i >= len(p):
                out.append(factor * q[i])
            else:
                out.append(p[i] + factor * q[i])
        return out

    def image(v):
        return tuple(add([zero] + p, sigma, p) if p else [] for p in v)

    xs, rs, ds = ([], []), ([], [one]), ([one], [])
    norm = rho[0]
    worst = zero
    for _ in range(ITERS):
        applied = image(ds)
        curvature, size = form(ds, applied)
        worst = jnp.maximum(worst, size / jnp.abs(curvature))
        bad = jnp.logical_not(size <= AMPLIFICATION_LIMIT * curvature)
        step = norm / curvature
        xs = tuple(add(p, step, q) for p, q in zip(xs, ds))
        rs = tuple(add(p, -step, q) for p, q in zip(rs, applied))
        after, size = form(rs, rs)
        bad = jnp.logical_or(bad, jnp.logical_not(size <= AMPLIFICATION_LIMIT * after))
        worst = jnp.where(bad, 2.0 * AMPLIFICATION_LIMIT, worst)
        ds = tuple(add(p, after / norm, q) for p, q in zip(rs, ds))
        norm = after
    rows = [a * inverse for a in xs[0] + xs[1]] + rs[0] + rs[1] + ds[0] + ds[1]
    for k, a in enumerate(rows):
        coef[k] = a
    flag[0] = jnp.where(jnp.max(worst) <= AMPLIFICATION_LIMIT, 1, 0).astype(jnp.int32)


def combine_kernel(x_ref, dc, rc, d1, d2, d3, d4, r1, r2, r3, coef, xo, ro, do):
    c = [coef[k] for k in range(25)]
    fields = (dc, d1, d2, d3, d4, rc, r1, r2, r3)
    to_x = dict(zip((0, 1, 2, 3, 5, 6, 7), c[0:7]))

    def row(x, _):
        for half in range(2):
            for k in range(8):
                at = (x * WY + 8 * half) * 8 + k
                b = [f[pl.ds(at, 8, stride=8), :] for f in fields]
                place = (x, slice(8 * half, 8 * half + 8), slice(128 * k, 128 * k + 128))
                value = x_ref[place]
                for i, a in to_x.items():
                    value = value + a * b[i]
                xo[place] = value
                for out, base in ((ro, 7), (do, 16)):
                    value = c[base] * b[0]
                    for i in range(1, 9):
                        value = value + c[base + i] * b[i]
                    out[place] = value
        return 0

    lax.fori_loop(0, WX, row, 0)


def spec(space=pltpu.VMEM):
    return pl.BlockSpec(memory_space=space)


def tiles_of(n):
    return jax.ShapeDtypeStruct((n * 8, 128), F32)


def estimate(flops, bytes_accessed):
    return pl.CostEstimate(flops=flops, bytes_accessed=bytes_accessed, transcendentals=0)


def moved(value, axis, step):
    count = lax.axis_size(axis)
    pairs = [(i, i + step) for i in range(count) if 0 <= i + step < count]
    return lax.ppermute(value, axis, pairs)


def total_over(rows, axis):
    return jnp.sum(lax.all_to_all(rows, axis, 0, 0, tiled=True), axis=0, keepdims=True)


def per_device(
    iterate,
    residual,
    direction,
    brain_mask,
    dictionary,
    spatial_weight,
    angular_weight,
    orient_offsets,
):
    cells = WX * WY
    dc, rc, mrow, ylo, yhi, xlo, xhi = pl.pallas_call(
        pack_kernel,
        out_shape=(
            tiles_of(cells), tiles_of(cells), tiles_of(2), tiles_of(Y_TILES),
            tiles_of(Y_TILES), tiles_of(ROW_TILES), tiles_of(ROW_TILES),
        ),
        in_specs=[spec()] * 3,
        out_specs=[spec()] * 7,
        cost_estimate=estimate(0, 4 << 20),
        name="pack",
    )(direction, residual, brain_mask)

    yl, yr = moved(yhi, "gy", 1), moved(ylo, "gy", -1)
    xlo, xhi = pl.pallas_call(
        corner_kernel,
        out_shape=(tiles_of(ROW_TILES),) * 2,
        in_specs=[spec(pltpu.HBM)] * 4,
        out_specs=[spec(pltpu.HBM)] * 2,
        scratch_shapes=[pltpu.SemaphoreType.DMA],
        input_output_aliases={2: 0, 3: 1},
        cost_estimate=estimate(0, 1 << 20),
        name="corners",
    )(yl, yr, xlo, xhi)
    xl, xr = moved(xhi, "gx", 1), moved(xlo, "gx", -1)

    weight_row = jnp.tile(spatial_weight, 2)[None, :]
    offset_rows = jnp.tile(orient_offsets.T, (1, 2))
    par = pl.pallas_call(
        weights_kernel,
        out_shape=jax.ShapeDtypeStruct((152, 256), F32),
        in_specs=[spec()] * 4,
        out_specs=spec(),
        cost_estimate=estimate(4 << 20, 1 << 19),
        name="weights",
    )(dictionary, angular_weight, angular_weight.T, weight_row)

    own = jax.ShapeDtypeStruct((WX, WY, 8, 128), F32)
    frame = pltpu.VMEM((FX, FY, 8, 128), F32)
    as_tiles = lambda a: a.reshape(-1, 8, 128)
    as_field = lambda a: a.reshape(WX, WY, 8, 128)
    outs = pl.pallas_call(
        krylov_kernel,
        out_shape=(own,) * 7 + (jax.ShapeDtypeStruct((16, 128), F32),),
        in_specs=[spec()] * 6 + [spec(pltpu.HBM)] * 3,
        out_specs=[spec(pl.ANY)] * 7 + [spec()],
        scratch_shapes=[frame] * 9
        + [
            pltpu.VMEM((FX * FY * 8, 128), F32),
            frame,
            frame,
            pltpu.VMEM((12, 8, 128), F32),
            pltpu.VMEM((FX * FY, 128), F32),
            pltpu.VMEM((Y_TILES, 8, 128), F32),
            pltpu.VMEM((Y_TILES, 8, 128), F32),
            pltpu.VMEM((2, 8, 128), F32),
            pltpu.VMEM((256, 256), BF16),
            pltpu.VMEM((256, 256), BF16),
            pltpu.SemaphoreType.DMA,
            pltpu.SemaphoreType.DMA,
        ],
        compiler_params=pltpu.CompilerParams(vmem_limit_bytes=40 << 20),
        cost_estimate=estimate(8 << 30, 8 << 20),
        name="krylov",
    )(
        as_field(dc), as_field(rc), as_tiles(xl), as_tiles(xr), offset_rows, par,
        as_tiles(yl), as_tiles(yr), as_tiles(mrow),
    )
    basis, part = outs[:7], outs[7]

    first = total_over(part, "gy")
    sums = lax.all_to_all(jnp.broadcast_to(first, (16, 128)), "gx", 0, 0, tiled=True)
    coef, flag = pl.pallas_call(
        scalars_kernel,
        out_shape=(
            jax.ShapeDtypeStruct((25, 8, 128), F32),
            jax.ShapeDtypeStruct((1,), jnp.int32),
        ),
        in_specs=[spec()] * 2,
        out_specs=[spec(), spec(pltpu.SMEM)],
        name="scalars",
    )(sums, par)

    def from_basis():
        return tuple(
            pl.pallas_call(
                combine_kernel,
                out_shape=(jax.ShapeDtypeStruct(iterate.shape, F32),) * 3,
                in_specs=[spec()] * 11,
                out_specs=[spec()] * 3,
                name="combine",
            )(iterate, dc, rc, *[b.reshape(-1, 128) for b in basis], coef)
        )

    def from_start():
        return plain_recurrence(
            iterate, residual, direction, brain_mask, dictionary, spatial_weight,
            angular_weight, orient_offsets,
        )

    return lax.cond(flag[0] == 1, from_basis, from_start)


def solution(mesh):
    field = P("gx", "gy", None)
    in_specs = (field,) * 4 + (P(),) * 4
    return jax.shard_map(
        per_device, mesh=mesh, in_specs=in_specs, out_specs=(field,) * 3, check_vma=False
    )
```

```python
import functools

import jax
import jax.numpy as jnp
from jax import lax
from jax.experimental import pallas as pl
from jax.experimental.pallas import tpu as pltpu
from jax.sharding import PartitionSpec as P

ITERS = 4
AXES = ("gx", "gy")
AMPLIFICATION_LIMIT = 200.0
F32 = jnp.float32
BF16 = jnp.bfloat16

DIRECTIONS = [
    (0, 0, 1),
    (0, 1, -1),
    (0, 1, 0),
    (0, 1, 1),
    (1, -1, -1),
    (1, -1, 0),
    (1, -1, 1),
    (1, 0, -1),
    (1, 0, 0),
    (1, 0, 1),
    (1, 1, -1),
    (1, 1, 0),
    (1, 1, 1),
]

WX, WY = 8, 16
DEEP = 4
FX, FY = WX + 2 * DEEP, WY + 2 * DEEP
Y_TILES = WX * (DEEP + DEEP - 1) + 1
X_TILES = WY * (DEEP + DEEP - 1) + 2
C_TILES = DEEP * 2 * DEEP + (DEEP - 1) * 2 * (DEEP - 1) + 2
MOMENTS = 24


def padded_2(cells, sides, width):
    for axis, dim in sides:
        count = lax.axis_size(axis)
        ends = count - 1
        head = lax.slice_in_dim(cells, 0, width, axis=dim)
        tail = lax.slice_in_dim(cells, cells.shape[dim] - width, cells.shape[dim], axis=dim)
        cells = jnp.concatenate(
            [
                lax.ppermute(tail, axis, [(i, (i + 1) % count) for i in range(ends)]),
                cells,
                lax.ppermute(head, axis, [((i + 1) % count, i) for i in range(ends)]),
            ],
            axis=dim,
        )
    return cells


def angular_matrix(angular_weight):
    symmetric = 0.5 * (angular_weight + angular_weight.T)
    channels = symmetric.shape[0]
    coupling = symmetric * (1.0 - jnp.eye(channels, dtype=jnp.float32))
    return jnp.diag(jnp.sum(coupling, axis=1)) - coupling


def channel_selector(orient_offsets):
    table = jnp.array(DIRECTIONS, dtype=jnp.int32)
    hits = jnp.all(orient_offsets[None, :, :] == table[:, None, :], axis=-1)
    return hits.astype(jnp.float32)


def neighbour_sum(extended, selector, width_x, width_y, depth, channels):
    padded = jnp.pad(extended, ((0, 0), (0, 0), (channels, channels)))
    running_sum = jnp.zeros((width_x, width_y, depth), jnp.float32)
    slices = depth // channels
    for number in range(len(DIRECTIONS)):
        step_x, step_y, step_z = DIRECTIONS[number]
        forward = padded[
            1 + step_x : 1 + step_x + width_x,
            1 + step_y : 1 + step_y + width_y,
            channels + step_z * channels : channels + step_z * channels + depth,
        ]
        backward = padded[
            1 - step_x : 1 - step_x + width_x,
            1 - step_y : 1 - step_y + width_y,
            channels - step_z * channels : channels - step_z * channels + depth,
        ]
        running_sum = running_sum + jnp.tile(selector[number], slices) * (forward + backward)
    return running_sum


def apply_operator(field_data, brain_mask, dictionary, spatial_rows, angular_full, selector):
    extended = padded_2(field_data, (("gx", 0), ("gy", 1)), 1)
    width_x, width_y, depth = field_data.shape
    channels = dictionary.shape[1]
    flattened = field_data.reshape(-1, channels)
    dot = functools.partial(
        jnp.dot, precision=lax.Precision.HIGHEST, preferred_element_type=jnp.float32
    )
    back_proj = dot(dot(flattened, dictionary.T), dictionary)
    mask_rows = brain_mask.reshape(-1).astype(jnp.float32)
    data_term = (back_proj * mask_rows[:, None]).reshape(width_x, width_y, depth)
    angular_term = dot(flattened, angular_full).reshape(width_x, width_y, depth)
    neighbours = neighbour_sum(extended, selector, width_x, width_y, depth, channels)
    return data_term + angular_term + spatial_rows * (2.0 * field_data - neighbours)


def plain_recurrence(
    iterate, residual, direction, brain_mask, dictionary, spatial_weight, angular_weight, offsets
):
    angular_full = angular_matrix(angular_weight)
    selector = channel_selector(offsets)
    spatial_rows = jnp.tile(spatial_weight, iterate.shape[2] // dictionary.shape[1])

    def step(_, state):
        iterate, residual, direction, norm_now = state
        images = apply_operator(
            direction, brain_mask, dictionary, spatial_rows, angular_full, selector
        )
        curvature = lax.psum(jnp.sum(direction * images), AXES)
        step_length = norm_now / curvature
        iterate = iterate + step_length * direction
        residual = residual - step_length * images
        norm_next = lax.psum(jnp.sum(residual * residual), AXES)
        direction = residual + norm_next / norm_now * direction
        return iterate, residual, direction, norm_next

    norm = lax.psum(jnp.sum(residual * residual), AXES)
    state = lax.fori_loop(0, ITERS, step, (iterate, residual, direction, norm))
    return state[:3]


def pack_kernel(d_ref, r_ref, m_ref, dc, rc, mrow, ylo, yhi, xlo, xhi):
    for src, dst in ((d_ref, dc), (r_ref, rc)):
        for x in range(WX):
            for half in range(2):
                for k in range(8):
                    tile = src[x, 8 * half : 8 * half + 8, 128 * k : 128 * k + 128]
                    dst[pl.ds((x * WY + 8 * half) * 8 + k, 8, stride=8), :] = tile
    for y in range(WY):
        lane = 16 * (y % 8)
        mrow[8 * (y // 8) : 8 * (y // 8) + 8, lane : lane + 16] = m_ref[:, y, :].astype(F32)
    base = 8 * WX * DEEP
    for x in range(WX):
        row = x * WY * 8
        for src, wide, at in ((dc, DEEP, 0), (rc, DEEP - 1, base)):
            n = 8 * wide
            ylo[at + x * n : at + x * n + n, :] = src[row : row + n, :]
            yhi[at + x * n : at + x * n + n, :] = src[row + WY * 8 - n : row + WY * 8, :]
    last = 8 * (Y_TILES - 1)
    ylo[last:, :] = mrow[0:8, :]
    yhi[last:, :] = mrow[8:16, :]
    at = 0
    for src, wide in ((dc, DEEP), (rc, DEEP - 1)):
        n = 8 * WY * wide
        xlo[at : at + n, :] = src[0:n, :]
        xhi[at : at + n, :] = src[8 * WX * WY - n :, :]
        at += n
    xlo[at:, :] = mrow[...]
    xhi[at:, :] = mrow[...]


def corner_kernel(left, right, clo, chi):
    at = 0
    base = 0
    for wide in (DEEP, DEEP - 1):
        n = 8 * wide
        for i in range(wide):
            for out, x in ((clo, i), (chi, WX - wide + i)):
                out[at : at + n, :] = left[base + x * n : base + x * n + n, :]
                out[at + n : at + 2 * n, :] = right[base + x * n : base + x * n + n, :]
            at += 2 * n
        base += WX * n
    for out in (clo, chi):
        out[at : at + 8, :] = left[base : base + 8, :]
        out[at + 8 : at + 16, :] = right[base : base + 8, :]


def weights_kernel(dict_ref, ang_ref, angt_ref, sw_ref, w_hi, w_lo, par, wide):
    dictionary = dict_ref[...]
    gram = lax.dot_general(
        dictionary,
        dictionary,
        (((0,), (0,)), ((), ())),
        precision=lax.Precision.HIGHEST,
        preferred_element_type=F32,
    )
    row = lax.broadcasted_iota(jnp.int32, (64, 64), 0)
    col = lax.broadcasted_iota(jnp.int32, (64, 64), 1)
    same = row == col
    coupling = jnp.where(same, 0.0, 0.5 * (ang_ref[...] + angt_ref[...]))
    degree = jnp.sum(coupling, axis=0, keepdims=True)
    weight = sw_ref[:, 0:64]
    angular = jnp.where(same, degree, 0.0) - coupling
    size = jnp.sum(jnp.abs(gram), axis=0, keepdims=True) + 2.0 * degree + 4.0 * weight
    scale = jnp.max(size, axis=1, keepdims=True)
    centre = jnp.sum(jnp.where(same, gram, 0.0), axis=0, keepdims=True) + degree + 2.0 * weight
    shift = jnp.sum(centre, axis=1, keepdims=True) * (1.0 / 64.0)
    inverse = 1.0 / scale
    first = gram * inverse
    second = (angular + jnp.where(same, 2.0 * weight - shift, 0.0)) * inverse
    wide[...] = jnp.zeros_like(wide)
    for half in range(2):
        at = 64 * half
        wide[at : at + 64, at : at + 64] = first
        wide[at : at + 64, 128 + at : 128 + at + 64] = second
    full = wide[...]
    high = full.astype(BF16)
    low = (full - high.astype(F32)).astype(BF16)
    w_hi[0:128, :] = high
    w_hi[128:256, :] = high
    w_lo[0:128, :] = low
    w_lo[128:256, :] = low
    par[0:8, :] = jnp.broadcast_to(sw_ref[...] * inverse, (8, 128))
    par[8:16, :] = jnp.broadcast_to(scale, (8, 128))
    par[16:24, :] = jnp.broadcast_to(shift, (8, 128))


def krylov_kernel(
    dc, rc, mrow, yl, yr, xl, xr, cl, cr, w_hi, w_lo, par, off,
    d1o, d2o, d3o, d4o, r1o, r2o, r3o, part,
    d0, d1, d2, d3, d4, r0, r1, r2, r3, me, qf, qb, tiles, lhs, in_sem, out_sem,
):
    copies = []

    def fetch(src, dst):
        copy = pltpu.make_async_copy(src, dst, in_sem)
        copy.start()
        copies.append(copy)

    own_x, own_y = pl.ds(DEEP, WX), pl.ds(DEEP, WY)
    fetch(dc, d0.at[own_x, own_y])
    fetch(rc, r0.at[own_x, own_y])
    for wide, field, base, xbase, cbase in (
        (DEEP, d0, 0, 0, 0),
        (DEEP - 1, r0, WX * DEEP, WY * DEEP, 2 * DEEP * DEEP),
    ):
        lo, hi_y, hi_x = DEEP - wide, DEEP + WY, DEEP + WX
        for x in range(WX):
            fetch(yl.at[pl.ds(base + wide * x, wide)], field.at[DEEP + x, pl.ds(lo, wide)])
            fetch(yr.at[pl.ds(base + wide * x, wide)], field.at[DEEP + x, pl.ds(hi_y, wide)])
        for i in range(wide):
            for block, corner, x in ((xl, cl, lo + i), (xr, cr, hi_x + i)):
                fetch(block.at[pl.ds(xbase + WY * i, WY)], field.at[x, own_y])
                at = cbase + 2 * wide * i
                fetch(corner.at[pl.ds(at, wide)], field.at[x, pl.ds(lo, wide)])
                fetch(corner.at[pl.ds(at + wide, wide)], field.at[x, pl.ds(hi_y, wide)])
    fetch(yl.at[pl.ds(Y_TILES - 1, 1)], tiles.at[pl.ds(0, 1)])
    fetch(mrow, tiles.at[pl.ds(1, 2)])
    fetch(yr.at[pl.ds(Y_TILES - 1, 1)], tiles.at[pl.ds(3, 1)])
    for at, block, corner in ((4, xl, cl), (8, xr, cr)):
        fetch(corner.at[pl.ds(C_TILES - 2, 1)], tiles.at[pl.ds(at, 1)])
        fetch(block.at[pl.ds(X_TILES - 2, 2)], tiles.at[pl.ds(at + 1, 2)])
        fetch(corner.at[pl.ds(C_TILES - 1, 1)], tiles.at[pl.ds(at + 3, 1)])

    sub = lax.broadcasted_iota(jnp.int32, (8, 128), 0)
    lane = lax.broadcasted_iota(jnp.int32, (8, 128), 1)
    off_x = jnp.broadcast_to(off[0:1, :], (8, 128))
    off_y = jnp.broadcast_to(off[1:2, :], (8, 128))
    off_z = jnp.broadcast_to(off[2:3, :], (8, 128))
    lower = lane < 64
    flat_z = off_z == 0
    direct = jnp.logical_or(
        jnp.logical_and(lower, off_z == 1), jnp.logical_and(lane >= 64, off_z == -1)
    )
    edge = jnp.logical_or(
        jnp.logical_and(lower, sub == 0), jnp.logical_and(lane >= 64, sub == 7)
    )
    inside = jnp.where(edge, 0.0, 1.0).astype(F32)
    y_minus, y_plus, x_step = off_y == -1, off_y == 1, off_x == 1
    weight = par[0:8, :]

    for copy in copies:
        copy.wait()

    for frame_y in range(1, FY - 1):
        y = frame_y - DEEP + 8
        group, amount = y // 8, 16 * (y % 8)
        column = jnp.concatenate(
            [tiles[4 + group][4:8], tiles[group], tiles[8 + group][0:4]], axis=0
        )
        if amount:
            column = pltpu.roll(column, 128 - amount, 1)
        lhs[pl.ds(frame_y, FX, stride=FY), :] = column
    slots = lhs[...].astype(BF16)
    z_row = lax.broadcasted_iota(jnp.int32, (128, 128), 0)
    z_lane = lax.broadcasted_iota(jnp.int32, (128, 128), 1) // 64
    for k in range(8):
        spread = jnp.where(z_row == 2 * k + z_lane, 1.0, 0.0).astype(BF16)
        me[pl.ds(k, FX * FY, stride=8), :] = jnp.dot(
            slots, spread, preferred_element_type=F32
        )

    gx, gy = lax.axis_index("gx"), lax.axis_index("gy")
    ends_x, ends_y = lax.axis_size("gx") - 1, lax.axis_size("gy") - 1

    def operator(src, dst, depth):
        lo, wide = DEEP - depth, WY + 2 * depth
        inner = wide - 2

        def shift_row(x, _):
            v = src[x, pl.ds(lo, wide)]
            rot = pltpu.roll(v, 64, 2)
            far = jnp.where(lower, pltpu.roll(rot, 1, 1), pltpu.roll(rot, 7, 1)) * inside
            u = jnp.where(flat_z, v, jnp.where(direct, rot, far))
            w = jnp.where(flat_z, v, jnp.where(direct, far, rot))
            qf[x, pl.ds(lo + 1, inner)] = jnp.where(
                y_minus, u[:-2], jnp.where(y_plus, u[2:], u[1:-1])
            )
            qb[x, pl.ds(lo + 1, inner)] = jnp.where(
                y_minus, w[2:], jnp.where(y_plus, w[:-2], w[1:-1])
            )
            return 0

        lax.fori_loop(lo, FX - lo, shift_row, 0)

        def combine_row(x, _):
            cols = pl.ds(lo + 1, inner)
            v = src[x, cols].reshape(inner * 8, 128)
            high = v.astype(BF16)
            low = (v - high.astype(F32)).astype(BF16)
            both = jnp.concatenate([high, low], axis=1)
            prod = jnp.dot(both, w_hi[...], preferred_element_type=F32)
            prod = prod + jnp.dot(both, w_lo[...], preferred_element_type=F32)
            near = jnp.where(x_step, qf[x + 1, cols], qf[x, cols])
            near = near + jnp.where(x_step, qb[x - 1, cols], qb[x, cols])
            data = prod[:, 0:128].reshape(inner, 8, 128)
            rest = prod[:, 128:256].reshape(inner, 8, 128)
            start = pl.multiple_of((x * FY + lo + 1) * 8, 8)
            mask = me[pl.ds(start, inner * 8), :].reshape(inner, 8, 128)
            dst[x, cols] = mask * data + rest - weight * near
            return 0

        lax.fori_loop(lo + 1, FX - lo - 1, combine_row, 0, unroll=2)

        border = depth - 1
        if border:
            zero_rows = jnp.zeros((border, inner, 8, 128), F32)
            zero_cols = jnp.zeros((WX + 2 * border, border, 8, 128), F32)
            rows, cols = pl.ds(lo + 1, FX - 2 * lo - 2), pl.ds(lo + 1, inner)

            @pl.when(gx == 0)
            def _():
                dst[pl.ds(lo + 1, border), cols] = zero_rows

            @pl.when(gx == ends_x)
            def _():
                dst[pl.ds(DEEP + WX, border), cols] = zero_rows

            @pl.when(gy == 0)
            def _():
                dst[rows, pl.ds(lo + 1, border)] = zero_cols

            @pl.when(gy == ends_y)
            def _():
                dst[rows, pl.ds(DEEP + WY, border)] = zero_cols

    stores = []

    def put(src, dst):
        copy = pltpu.make_async_copy(src.at[own_x, own_y], dst, out_sem)
        copy.start()
        stores.append(copy)

    for src, dst, out, depth in (
        (d0, d1, d1o, 4),
        (d1, d2, d2o, 3),
        (r0, r1, r1o, 3),
        (d2, d3, d3o, 2),
        (r1, r2, r2o, 2),
        (d3, d4, d4o, 1),
        (r2, r3, r3o, 1),
    ):
        operator(src, dst, depth)
        put(dst, out)

    ds, rs = (d0, d1, d2, d3, d4), (r0, r1, r2, r3)
    pairs = [(ds[k // 2], ds[k - k // 2]) for k in range(9)]
    pairs += [(rs[min(k // 2, 3)], ds[k - min(k // 2, 3)]) for k in range(8)]
    pairs += [(rs[k // 2], rs[k - k // 2]) for k in range(7)]

    def accumulate(i, acc):
        x, y = DEEP + i // 2, DEEP + 8 * (i % 2)
        cols = pl.ds(y, 8)
        loaded = {id(f): f[x, cols] for f in ds + rs}
        return tuple(
            a + jnp.sum(loaded[id(f)] * loaded[id(g)], axis=0)
            for a, (f, g) in zip(acc, pairs)
        )

    zero = jnp.zeros((8, 128), F32)
    acc = lax.fori_loop(0, 2 * WX, accumulate, (zero,) * MOMENTS)
    total = zero[0:1, :]
    lane_row = lax.broadcasted_iota(jnp.int32, (1, 128), 1)
    for k, a in enumerate(acc):
        value = jnp.sum(jnp.sum(a, axis=0, keepdims=True), axis=1, keepdims=True)
        total = jnp.where(lane_row == k, value, total)
    part[...] = jnp.broadcast_to(total, part.shape)
    for copy in stores:
        copy.wait()


def scalars_kernel(sums, par, coef, flag):
    row = jnp.sum(sums[...], axis=0, keepdims=True)
    moment = [jnp.broadcast_to(row[:, k : k + 1], (8, 128)) for k in range(MOMENTS)]
    mu, nu, rho = moment[0:9], moment[9:17], moment[17:24]
    scale = par[8:16, :]
    inverse = 1.0 / scale
    sigma = par[16:24, :] * inverse
    one, zero = jnp.ones((8, 128), F32), jnp.zeros((8, 128), F32)

    def product(p, q):
        out = [None] * max(len(p) + len(q) - 1, 0)
        for i, a in enumerate(p):
            for j, b in enumerate(q):
                out[i + j] = a * b if out[i + j] is None else out[i + j] + a * b
        return out

    def form(v, w):
        crossed = product(v[0], w[1]), product(w[0], v[1])
        total, size = zero, zero
        for c, m in ((product(v[0], w[0]), mu), (product(v[1], w[1]), rho)):
            for a, b in zip(c, m):
                total, size = total + a * b, size + jnp.abs(a * b)
        for a, b, m in zip(crossed[0], crossed[1], nu):
            total, size = total + (a + b) * m, size + (jnp.abs(a) + jnp.abs(b)) * jnp.abs(m)
        return total, size

    def add(p, factor, q):
        out = []
        for i in range(max(len(p), len(q))):
            if i >= len(q):
                out.append(p[i])
            elif i >= len(p):
                out.append(factor * q[i])
            else:
                out.append(p[i] + factor * q[i])
        return out

    def image(v):
        return tuple(add([zero] + p, sigma, p) if p else [] for p in v)

    xs, rs, ds = ([], []), ([], [one]), ([one], [])
    norm = rho[0]
    worst = zero
    for _ in range(ITERS):
        applied = image(ds)
        curvature, size = form(ds, applied)
        worst = jnp.maximum(worst, size / jnp.abs(curvature))
        bad = jnp.logical_not(size <= AMPLIFICATION_LIMIT * curvature)
        step = norm / curvature
        xs = tuple(add(p, step, q) for p, q in zip(xs, ds))
        rs = tuple(add(p, -step, q) for p, q in zip(rs, applied))
        after, size = form(rs, rs)
        bad = jnp.logical_or(bad, jnp.logical_not(size <= AMPLIFICATION_LIMIT * after))
        worst = jnp.where(bad, 2.0 * AMPLIFICATION_LIMIT, worst)
        ds = tuple(add(p, after / norm, q) for p, q in zip(rs, ds))
        norm = after
    rows = [a * inverse for a in xs[0] + xs[1]] + rs[0] + rs[1] + ds[0] + ds[1]
    for k, a in enumerate(rows):
        coef[k] = a
    flag[...] = jnp.where(worst <= AMPLIFICATION_LIMIT, 1, 0).astype(jnp.int32)


def combine_kernel(x_ref, dc, rc, d1, d2, d3, d4, r1, r2, r3, coef, xo, ro, do):
    c = [coef[k] for k in range(25)]
    fields = (dc, d1, d2, d3, d4, rc, r1, r2, r3)
    to_x = dict(zip((0, 1, 2, 3, 5, 6, 7), c[0:7]))

    def row(x, _):
        for half in range(2):
            for k in range(8):
                at = (x * WY + 8 * half) * 8 + k
                b = [f[pl.ds(at, 8, stride=8), :] for f in fields]
                place = (x, slice(8 * half, 8 * half + 8), slice(128 * k, 128 * k + 128))
                value = x_ref[place]
                for i, a in to_x.items():
                    value = value + a * b[i]
                xo[place] = value
                for out, base in ((ro, 7), (do, 16)):
                    value = c[base] * b[0]
                    for i in range(1, 9):
                        value = value + c[base + i] * b[i]
                    out[place] = value
        return 0

    lax.fori_loop(0, WX, row, 0)


def spec(space=pltpu.VMEM):
    return pl.BlockSpec(memory_space=space)


def tiles_of(n):
    return jax.ShapeDtypeStruct((n * 8, 128), F32)


def estimate(flops, bytes_accessed):
    return pl.CostEstimate(flops=flops, bytes_accessed=bytes_accessed, transcendentals=0)


def moved(value, axis, step):
    count = lax.axis_size(axis)
    pairs = [(i, i + step) for i in range(count) if 0 <= i + step < count]
    return lax.ppermute(value, axis, pairs)


def total_over(rows, axis):
    return jnp.sum(lax.all_to_all(rows, axis, 0, 0, tiled=True), axis=0, keepdims=True)


def per_device(
    iterate,
    residual,
    direction,
    brain_mask,
    dictionary,
    spatial_weight,
    angular_weight,
    orient_offsets,
):
    cells = WX * WY
    dc, rc, mrow, ylo, yhi, xlo, xhi = pl.pallas_call(
        pack_kernel,
        out_shape=(
            tiles_of(cells), tiles_of(cells), tiles_of(2), tiles_of(Y_TILES),
            tiles_of(Y_TILES), tiles_of(X_TILES), tiles_of(X_TILES),
        ),
        in_specs=[spec()] * 3,
        out_specs=[spec()] * 7,
        cost_estimate=estimate(0, 4 << 20),
        name="pack",
    )(direction, residual, brain_mask)

    yl, yr = moved(yhi, "gy", 1), moved(ylo, "gy", -1)
    xl, xr = moved(xhi, "gx", 1), moved(xlo, "gx", -1)
    clo, chi = pl.pallas_call(
        corner_kernel,
        out_shape=(tiles_of(C_TILES),) * 2,
        in_specs=[spec()] * 2,
        out_specs=[spec()] * 2,
        cost_estimate=estimate(0, 1 << 20),
        name="corners",
    )(yl, yr)
    cl, cr = moved(chi, "gx", 1), moved(clo, "gx", -1)

    weight_row = jnp.tile(spatial_weight, 2)[None, :]
    offset_rows = jnp.tile(orient_offsets.T, (1, 2))
    w_hi, w_lo, par = pl.pallas_call(
        weights_kernel,
        out_shape=(
            jax.ShapeDtypeStruct((256, 256), BF16),
            jax.ShapeDtypeStruct((256, 256), BF16),
            tiles_of(3),
        ),
        in_specs=[spec()] * 4,
        out_specs=[spec()] * 3,
        scratch_shapes=[pltpu.VMEM((128, 256), F32)],
        cost_estimate=estimate(4 << 20, 1 << 19),
        name="weights",
    )(dictionary, angular_weight, angular_weight.T, weight_row)

    own = jax.ShapeDtypeStruct((WX, WY, 8, 128), F32)
    frame = pltpu.VMEM((FX, FY, 8, 128), F32)
    as_tiles = lambda a: a.reshape(-1, 8, 128)
    as_field = lambda a: a.reshape(WX, WY, 8, 128)
    outs = pl.pallas_call(
        krylov_kernel,
        out_shape=(own,) * 7 + (jax.ShapeDtypeStruct((16, 128), F32),),
        in_specs=[spec(pl.ANY)] * 9 + [spec()] * 4,
        out_specs=[spec(pl.ANY)] * 7 + [spec()],
        scratch_shapes=[frame] * 9
        + [
            pltpu.VMEM((FX * FY * 8, 128), F32),
            frame,
            frame,
            pltpu.VMEM((12, 8, 128), F32),
            pltpu.VMEM((FX * FY, 128), F32),
            pltpu.SemaphoreType.DMA,
            pltpu.SemaphoreType.DMA,
        ],
        compiler_params=pltpu.CompilerParams(vmem_limit_bytes=40 << 20),
        cost_estimate=estimate(8 << 30, 8 << 20),
        name="krylov",
    )(
        as_field(dc), as_field(rc), as_tiles(mrow), as_tiles(yl), as_tiles(yr),
        as_tiles(xl), as_tiles(xr), as_tiles(cl), as_tiles(cr), w_hi, w_lo, par, offset_rows,
    )
    basis, part = outs[:7], outs[7]

    first = total_over(part, "gy")
    sums = lax.all_to_all(jnp.broadcast_to(first, (16, 128)), "gx", 0, 0, tiled=True)
    coef, flag = pl.pallas_call(
        scalars_kernel,
        out_shape=(
            jax.ShapeDtypeStruct((25, 8, 128), F32),
            jax.ShapeDtypeStruct((8, 128), jnp.int32),
        ),
        in_specs=[spec()] * 2,
        out_specs=[spec()] * 2,
        name="scalars",
    )(sums, par)

    def from_basis():
        return tuple(
            pl.pallas_call(
                combine_kernel,
                out_shape=(jax.ShapeDtypeStruct(iterate.shape, F32),) * 3,
                in_specs=[spec()] * 11,
                out_specs=[spec()] * 3,
                name="combine",
            )(iterate, dc, rc, *[b.reshape(-1, 128) for b in basis], coef)
        )

    def from_start():
        return plain_recurrence(
            iterate, residual, direction, brain_mask, dictionary, spatial_weight,
            angular_weight, orient_offsets,
        )

    return lax.cond(flag[0, 0] == 1, from_basis, from_start)


def solution(mesh):
    field = P("gx", "gy", None)
    in_specs = (field,) * 4 + (P(),) * 4
    return jax.shard_map(
        per_device, mesh=mesh, in_specs=in_specs, out_specs=(field,) * 3, check_vma=False
    )
```
